32 devices in a mesh: gx: 8 (over z, y), gy: 4 (over x, core).
Axes of the slice: x: 2, y: 2, z: 4, core: 2. Of those that a mesh axis runs over, the one named last changes fastest.
Arguments:
- inputs: bfloat16 [32, 32, 32, 128], P(None, 'gx', 'gy'), may hold values from -6 to 6
- diffusion: bfloat16 [32, 32, 128], P('gx', 'gy'), may hold values from 0.049804688 to 0.5
- spectral: bfloat16 [16, 16, 2, 32, 1024], P('gx', 'gy'), may hold values from -1 to 1
- pointwise: bfloat16 [32, 32], replicated, may hold values from -1 to 1
- offsets: float32 [32], replicated, may hold values from -1 to 1
Outputs:
- activated: bfloat16 [32, 32, 32, 128], P(None, 'gx', 'gy')
The draws below stay inside these ranges and needn't reach their ends.
All inputs are finite; a program needn't handle non-finite values.
Results may differ from the reference program's by a relative error of at most 0.006.
Values may be sent and summed in bfloat16 or wider, within the bound.
No kernel may reach another device: no remote copies, remote signals or barrier semaphores. Data moves between devices by JAX's collectives and lax.ppermute only.
A program may use at most 64 MiB of HBM per device.

```python
import math
import jax
import jax.numpy as jnp
from jax import lax

C = 32
MY = 16
MZ = 32
NZ = 128
MX = 16
NX = 32
NY = 32


def block_scale(own_key, shape, split, low, top_value):
    def one(position, shards_of):
        heights = jax.random.uniform(jax.random.fold_in(jax.random.fold_in(own_key, 6), position), (shards_of,), jnp.float32, low / len(split), top_value / len(split))
        return jnp.repeat(jnp.exp(heights), shape[position] // shards_of).reshape((-1,) + (1,) * (len(shape) - position - 1))

    loudness = one(*split[0])
    for cut in split[1:]:
        loudness = loudness * one(*cut)
    return loudness


def normal_values(rng, dims, scale, most, shards=(), kind=jnp.bfloat16):
    drawn = jax.random.normal(rng, dims, jnp.float32) * scale
    if len(shards) > 0:
        drawn = block_scale(rng, dims, shards, -0.22, 0.18) * drawn
    return jnp.clip(drawn, min=-most, max=most).astype(kind)


def setup_inputs(seed: int = 0) -> dict:
    seeds = jax.random.split(jax.random.key(seed), 6)
    return {
        "inputs": normal_values(seeds[0], (C, NX, NY, NZ), 1.0, 6.0, ((1, 8), (2, 4))),
        "diffusion": jnp.clip(jnp.exp(math.log(0.5) - 2.306499 * jax.random.uniform(seeds[1], (NX, NY, NZ), jnp.float32) ** block_scale(seeds[1], (NX, NY, NZ), ((0, 8), (1, 4)), -0.2, 0.2)), 0.049804688, 0.5).astype(jnp.bfloat16),
        "spectral": normal_values(seeds[2], (MX, MY, 2, C, C * MZ), C ** -0.5, 1.0, ((0, 8), (1, 4))),
        "pointwise": normal_values(seeds[3], (C, C), C ** -0.5, 1.0),
        "offsets": jnp.clip(jax.random.uniform(seeds[4], (C,), jnp.float32, -1.0, 1.0), -1.0, 1.0),
    }


def frequencies(modes):
    indices = jnp.arange(modes, dtype=jnp.int32)
    return jnp.where(indices < modes // 2, indices, indices - modes).astype(jnp.int32)

def phase_table(positions, waves, length, rotate):
    windings = positions[:, None] * waves[None, :] % length
    angles = 2.0 * math.pi / length * windings.astype(jnp.float32)
    cosine = jnp.cos(angles)
    sines = rotate * jnp.sin(angles)
    from_real = jnp.stack([cosine, sines], axis=-1)
    from_imag = jnp.stack([-sines, cosine], axis=-1)
    return jnp.stack([from_real, from_imag], axis=1)

def z_tables(length_z, modes_z):
    positions = jnp.arange(length_z, dtype=jnp.int32)
    waves = jnp.arange(modes_z, dtype=jnp.int32)
    forward = phase_table(positions, waves, length_z, -1.0)[:, 0, :, :]
    forward = jnp.transpose(forward, (0, 2, 1)).reshape(length_z, 2 * modes_z)
    backward = phase_table(positions, waves, length_z, 1.0)[:, :, :, 0]
    backward = jnp.transpose(backward, (1, 2, 0)).reshape(2 * modes_z, length_z)
    return (forward.astype(jnp.bfloat16), backward)

def contract(u_part, w_part):
    return jnp.einsum('cakz,akcoz->oakz', u_part, w_part, precision=lax.Precision.HIGHEST)

def reference(inputs, diffusion, spectral, pointwise, offsets):
    highest = lax.Precision.HIGHEST
    z_forward, z_inverse = z_tables(NZ, MZ)
    z_spectrum = jnp.dot(inputs.reshape(-1, NZ), z_forward, preferred_element_type=jnp.float32)
    z_spectrum = z_spectrum.reshape(C, NX, NY, 2, MZ)
    y_table = phase_table(jnp.arange(NY, dtype=jnp.int32), frequencies(MY), NY, -1.0)
    y_partial = jnp.einsum('cxyqz,yqkp->cxkpz', z_spectrum, y_table, precision=highest)
    x_table = phase_table(jnp.arange(NX, dtype=jnp.int32), frequencies(MX), NX, -1.0)
    modes = jnp.einsum('cxkqz,xqap->cakpz', y_partial, x_table, precision=highest)
    modes = modes * (1.0 / math.sqrt(NX * NY * NZ))
    weights = spectral.astype(jnp.float32).reshape(MX, MY, 2, C, C, MZ)
    w_real = weights[:, :, 0]
    w_imag = weights[:, :, 1]
    u_real = modes[:, :, :, 0]
    u_imag = modes[:, :, :, 1]
    y_real = contract(u_real, w_real) - contract(u_imag, w_imag)
    y_imag = contract(u_real, w_imag) + contract(u_imag, w_real)
    mixed = jnp.stack([y_real, y_imag], axis=3).astype(jnp.bfloat16)
    x_inverse = jnp.transpose(phase_table(jnp.arange(NX, dtype=jnp.int32), frequencies(MX), NX, 1.0), (2, 1, 0, 3))
    y_inverse = jnp.transpose(phase_table(jnp.arange(NY, dtype=jnp.int32), frequencies(MY), NY, 1.0), (2, 1, 0, 3))
    back_x = jnp.einsum('oakqz,aqxp->oxkpz', mixed.astype(jnp.float32), x_inverse, precision=highest)
    spatial = jnp.einsum('oxkqz,kqyp->oxypz', back_x, y_inverse, precision=highest)
    inverse_scale = 1.0 / math.sqrt(MX * MY * MZ)

    def x_slice(index_x):
        local_modes = lax.dynamic_slice_in_dim(spatial, index_x, 1, 1).reshape(-1, 2 * MZ)
        spectral_out = jnp.dot(local_modes, z_inverse, precision=highest, preferred_element_type=jnp.float32)
        spectral_out = spectral_out.reshape(C, NY, NZ) * inverse_scale
        values = lax.dynamic_slice_in_dim(inputs, index_x, 1, 1).reshape(C, NY, NZ)
        mixing = jnp.dot(pointwise, values.reshape(C, -1), preferred_element_type=jnp.float32).reshape(C, NY, NZ)
        widened = values.astype(jnp.float32)
        padded = jnp.pad(widened, ((0, 0), (0, 0), (1, 1)))
        curvature = padded[:, :, 2:] - 2.0 * widened + padded[:, :, :-2]
        local_coeff = lax.dynamic_slice_in_dim(diffusion, index_x, 1, 0).reshape(NY, NZ).astype(jnp.float32)
        summed_all = spectral_out + mixing + local_coeff[None] * curvature + offsets[:, None, None]
        return jax.nn.gelu(summed_all, approximate=False).astype(jnp.bfloat16)
    slices = lax.map(x_slice, jnp.arange(NX, dtype=jnp.int32))
    return jnp.transpose(slices, (1, 0, 2, 3))
```

```python
import functools
import math

import jax
import jax.numpy as jnp
import numpy as np
from jax import lax
from jax.experimental import pallas as pl
from jax.experimental.pallas import tpu as pltpu
from jax.sharding import PartitionSpec as P

LANES = 128
GROUP = LANES // 2


def signed(modes):
    index = np.arange(modes)
    return np.where(index < modes // 2, index, index - modes)


class Plan:
    def __init__(self, ranks_x, ranks_y, channels, cx, cy, nz, kxd, kyd, mz):
        self.rx, self.ry = ranks_x, ranks_y
        self.c, self.cx, self.cy, self.nz = channels, cx, cy, nz
        self.kxd, self.kyd, self.mz = kxd, kyd, mz
        self.nx, self.ny = cx * ranks_x, cy * ranks_y
        self.mx, self.my = kxd * ranks_x, kyd * ranks_y
        self.devices = ranks_x * ranks_y
        self.slices = self.devices // channels
        self.mzs = mz // self.slices
        self.half = cx // 2
        self.rows = self.half * cy
        self.owned = kxd * kyd
        assert self.devices == self.slices * channels
        assert nz == LANES and 4 * mz == LANES and channels * mz % LANES == 0

    def z_forward(self):
        z = np.arange(self.nz)[:, None]
        kz = np.arange(self.mz)[None, :]
        angle = 2.0 * np.pi / self.nz * (z * kz % self.nz)
        table = np.zeros((self.slices, 2, self.nz, LANES), np.float32)
        for s in range(self.slices):
            part = slice(s * self.mzs, (s + 1) * self.mzs)
            for h in range(2):
                at = h * GROUP
                table[s, h, :, at : at + self.mzs] = np.cos(angle)[:, part]
                table[s, h, :, at + self.mz : at + self.mz + self.mzs] = -np.sin(angle)[:, part]
        return table.reshape(self.slices, 2 * self.nz, LANES)

    def z_inverse(self):
        kz = np.arange(self.mz)[:, None]
        z = np.arange(self.nz)[None, :]
        angle = 2.0 * np.pi / self.nz * (z * kz % self.nz)
        scale = 1.0 / math.sqrt(self.mx * self.my * self.mz)
        table = np.zeros((self.slices, 2, LANES, self.nz), np.float32)
        for s in range(self.slices):
            part = slice(s * self.mzs, (s + 1) * self.mzs)
            for h in range(2):
                at = h * GROUP
                table[s, h, at : at + self.mzs] = scale * np.cos(angle)[part]
                table[s, h, at + self.mz : at + self.mz + self.mzs] = -scale * np.sin(angle)[part]
        return table

    def turns(self):
        kx, ky = signed(self.mx), signed(self.my)
        mode_x = kx.reshape(self.rx, 1, self.kxd, 1)
        mode_y = ky.reshape(1, self.ry, 1, self.kyd)
        shape = (self.rx, self.ry, self.kxd, self.kyd)
        mode_x = np.broadcast_to(mode_x, shape).reshape(-1)
        mode_y = np.broadcast_to(mode_y, shape).reshape(-1)
        x = (np.arange(self.rx)[:, None] * self.cx + np.arange(self.half)).reshape(
            self.rx, 1, self.half, 1
        )
        y = np.arange(self.ny).reshape(1, self.ry, 1, self.cy)
        shape = (self.rx, self.ry, self.half, self.cy)
        x = np.broadcast_to(x, shape).reshape(-1)
        y = np.broadcast_to(y, shape).reshape(-1)
        return mode_x, mode_y, x, y

    def angles(self, shift):
        mode_x, mode_y, x, y = self.turns()
        along_x = mode_x[:, None] * (x[None, :] + shift) % self.nx
        along_y = mode_y[:, None] * y[None, :] % self.ny
        return 2.0 * np.pi * (along_x / self.nx + along_y / self.ny)

    def forward(self):
        angle = self.angles(0)
        return np.concatenate([np.cos(angle), np.sin(angle)], axis=0)

    def shift_phase(self):
        mode_x = self.turns()[0]
        angle = 2.0 * np.pi * (mode_x * self.half % self.nx) / self.nx
        scale = 1.0 / math.sqrt(self.nx * self.ny * self.nz)
        sign = np.where(np.arange(LANES) % GROUP < self.mz, 1.0, -1.0)
        cosine = np.cos(angle)[:, None] * np.ones(LANES)
        sine = np.sin(angle)[:, None] * sign
        return (np.stack([cosine, sine]) * scale).astype(np.float32), scale

    def backward(self):
        halves = []
        for h in range(2):
            angle = self.angles(h * self.half).T
            halves.append(np.concatenate([np.cos(angle), np.sin(angle)], axis=1))
        return np.concatenate(halves, axis=0)

    def spread(self):
        per = LANES // self.mz
        table = np.zeros((self.slices, LANES, 2 * LANES), np.float32)
        for s in range(self.slices):
            for q in range(2):
                for k in range(self.mzs):
                    for o in range(per):
                        table[s, q * self.mz + k, q * LANES + o * self.mz + s * self.mzs + k] = 1
        return table

    def pick(self):
        per = LANES // self.mz
        table = np.zeros((per, self.slices, 2 * LANES, LANES), np.float32)
        for o in range(per):
            for s in range(self.slices):
                for q in range(2):
                    for k in range(self.mzs):
                        row = q * LANES + o * self.mz + s * self.mzs + k
                        for h in range(2):
                            table[o, s, row, h * GROUP + q * self.mz + k] = 1
        return table


def dot(a, b):
    return jnp.dot(a, b, preferred_element_type=jnp.float32)


def lanes_of(shape):
    return lax.broadcasted_iota(jnp.int32, shape, len(shape) - 1)


def to_lines(plan, x_ref, f_ref, out_ref):
    half, c, cy = plan.half, plan.c, plan.cy
    x = x_ref[...]
    low = x[:, :half].reshape(c * plan.rows, LANES)
    high = x[:, half:].reshape(c * plan.rows, LANES)
    cells = jnp.concatenate([low, high], axis=1)
    for s in range(plan.slices):
        line = dot(cells, f_ref[s]).astype(jnp.bfloat16)
        out_ref[:, s] = line.reshape(c, plan.rows, LANES)


def to_modes(plan, x_ref, t_ref, phase_ref, out_ref):
    modes = plan.devices * plan.owned
    x = x_ref[...].reshape(plan.devices * plan.rows, LANES)
    turned = dot(t_ref[...], x)
    cosine, sine = turned[:modes], turned[modes:]
    real = lanes_of((modes, LANES)) % GROUP < plan.mz
    up = LANES - plan.mz
    u = cosine + jnp.where(real, pltpu.roll(sine, up, 1), -pltpu.roll(sine, plan.mz, 1))
    other = jnp.where(real, pltpu.roll(u, plan.mz, 1), pltpu.roll(u, up, 1))
    scale = plan.shift_phase()[1]
    whole = u * scale + phase_ref[0] * pltpu.roll(u, GROUP, 1) + phase_ref[1] * other
    out_ref[...] = whole.reshape(plan.devices, plan.owned, LANES).astype(jnp.bfloat16)


def mix(plan, u_ref, w_ref, spread_ref, pick_ref, out_ref, wide, sums):
    c, owned = plan.c, plan.owned
    blocks = c * plan.mz // LANES
    per = LANES // plan.mz
    u = u_ref[...]
    total = None
    for s in range(plan.slices):
        part = dot(u[:, s].reshape(c * owned, LANES), spread_ref[s])
        total = part if total is None else total + part
    wide[0] = total[:, :LANES]
    wide[1] = total[:, LANES:]
    for m in range(owned):
        u_real = wide[0, pl.ds(m, c, stride=owned), :]
        u_imag = wide[1, pl.ds(m, c, stride=owned), :]
        for j in range(blocks):
            at = pl.ds(j * LANES, LANES)
            w_real = w_ref[m, 0, :, at].astype(jnp.float32)
            w_imag = w_ref[m, 1, :, at].astype(jnp.float32)
            y_real = jnp.sum(w_real * u_real - w_imag * u_imag, axis=0, keepdims=True)
            y_imag = jnp.sum(w_real * u_imag + w_imag * u_real, axis=0, keepdims=True)
            sums[pl.ds(j * owned + m, 1), :LANES] = y_real
            sums[pl.ds(j * owned + m, 1), LANES:] = y_imag
    mixed = sums[...].astype(jnp.bfloat16)
    for o in range(per):
        for s in range(plan.slices):
            line = dot(mixed, pick_ref[o, s]).reshape(blocks, owned, LANES)
            out_ref[:, o, s] = line.astype(jnp.bfloat16)


def from_modes(plan, m_ref, t_ref, out_ref):
    modes = plan.devices * plan.owned
    cells = plan.devices * plan.rows
    m = m_ref[...].reshape(modes, LANES)
    real = lanes_of((modes, LANES)) % GROUP < plan.mz
    swapped = pltpu.roll(m.astype(jnp.float32), plan.mz, 1)
    swapped = jnp.where(real, -swapped, swapped).astype(jnp.bfloat16)
    both = jnp.concatenate([m, swapped], axis=0)
    turned = dot(t_ref[...], both)
    first = lanes_of((cells, LANES)) < GROUP
    out = jnp.where(first, turned[:cells], turned[cells:])
    out_ref[...] = out.reshape(plan.devices, plan.rows, LANES).astype(jnp.bfloat16)


def local_terms(plan, x_ref, d_ref, p_ref, o_ref, out_ref):
    c, cy = plan.c, plan.cy
    size = c * cy
    row = lax.broadcasted_iota(jnp.int32, (size, c), 0) // cy
    pick = (row == lax.broadcasted_iota(jnp.int32, (size, c), 1)).astype(jnp.bfloat16)
    spread = dot(pick, p_ref[...]).astype(jnp.bfloat16)
    wide = lax.dot_general(spread, pick, (((1,), (1,)), ((), ())), preferred_element_type=jnp.float32)
    same = (
        lax.broadcasted_iota(jnp.int32, (size, size), 0) % cy
        == lax.broadcasted_iota(jnp.int32, (size, size), 1) % cy
    )
    mixer = jnp.where(same, wide, 0.0).astype(jnp.bfloat16)
    lane = lanes_of((size, LANES))
    for x in range(plan.cx):
        v = x_ref[:, x].reshape(size, LANES)
        mixing = dot(mixer, v)
        f = v.astype(jnp.float32)
        before = jnp.where(lane == 0, 0.0, pltpu.roll(f, 1, 1))
        after = jnp.where(lane == LANES - 1, 0.0, pltpu.roll(f, LANES - 1, 1))
        curvature = (before + after - 2.0 * f).reshape(c, cy, LANES)
        d = d_ref[x].astype(jnp.float32)
        out_ref[:, x] = mixing.reshape(c, cy, LANES) + d[None] * curvature + o_ref[...]


def finish(plan, s_ref, b_ref, z_ref, out_ref):
    c, half = plan.c, plan.half
    for h in range(2):
        total = None
        for s in range(plan.slices):
            part = dot(s_ref[:, s].reshape(c * plan.rows, LANES), z_ref[s, h])
            total = part if total is None else total + part
        v = total.reshape(c, half, plan.cy, LANES) + b_ref[:, h * half : (h + 1) * half]
        gelu = 0.5 * v * (1.0 + lax.erf(v * math.sqrt(0.5)))
        out_ref[:, h * half : (h + 1) * half] = gelu.astype(jnp.bfloat16)


def call(body, plan, out, scratch=(), flops=0, moved=0):
    return pl.pallas_call(
        functools.partial(body, plan),
        out_shape=out,
        scratch_shapes=list(scratch),
        cost_estimate=pl.CostEstimate(flops=flops, bytes_accessed=moved, transcendentals=0),
    )


def on_device(inputs, diffusion, spectral, pointwise, offsets):
    ranks_x = lax.axis_size("gx")
    ranks_y = lax.axis_size("gy")
    c, cx, cy, nz = inputs.shape
    kxd, kyd = spectral.shape[:2]
    plan = Plan(ranks_x, ranks_y, c, cx, cy, nz, kxd, kyd, spectral.shape[4] // c)
    axes = ("gx", "gy")
    bf16 = jnp.bfloat16
    d, s = plan.devices, plan.slices
    shape = jax.ShapeDtypeStruct
    exchange = functools.partial(lax.all_to_all, axis_name=axes, split_axis=0, concat_axis=0, tiled=True)

    def table(values):
        return jnp.asarray(np.asarray(values, np.float32).astype(bf16))

    lines = call(to_lines, plan, shape((c, s, plan.rows, LANES), bf16))(
        inputs, table(plan.z_forward())
    )
    lines = exchange(lines.reshape(d, plan.rows, LANES))
    base = call(
        local_terms, plan, shape((c, cx, cy, nz), jnp.float32), flops=10**9, moved=10**6
    )(inputs, diffusion, pointwise, jnp.broadcast_to(offsets[:, None, None], (c, cy, LANES)))
    phase = plan.shift_phase()[0]
    modes = call(to_modes, plan, shape((d, plan.owned, LANES), bf16))(
        lines, table(plan.forward()), jnp.asarray(phase)
    )
    modes = exchange(modes)
    mixed = call(
        mix,
        plan,
        shape((c * plan.mz // LANES, LANES // plan.mz, s, plan.owned, LANES), bf16),
        scratch=[
            pltpu.VMEM((2, c * plan.owned, LANES), jnp.float32),
            pltpu.VMEM((c * plan.mz // LANES * plan.owned, 2 * LANES), jnp.float32),
        ],
    )(
        modes.reshape(c, s, plan.owned, LANES),
        spectral.reshape(plan.owned, 2, c, c * plan.mz),
        table(plan.spread()),
        table(plan.pick()),
    )
    mixed = exchange(mixed.reshape(d, plan.owned, LANES))
    spatial = call(from_modes, plan, shape((d, plan.rows, LANES), bf16))(
        mixed, table(plan.backward())
    )
    spatial = exchange(spatial)
    return call(finish, plan, shape((c, cx, cy, nz), bf16))(
        spatial.reshape(c, s, plan.rows, LANES), base, table(plan.z_inverse())
    )


def solution(mesh):
    in_specs = (
        P(None, "gx", "gy", None),
        P("gx", "gy", None),
        P("gx", "gy", None, None, None),
        P(),
        P(),
    )
    out_specs = P(None, "gx", "gy", None)
    return jax.shard_map(
        on_device, mesh=mesh, in_specs=in_specs, out_specs=out_specs, check_vma=False
    )
```

```python
import functools
import math

import jax
import jax.numpy as jnp
import numpy as np
from jax import lax
from jax.experimental import pallas as pl
from jax.experimental.pallas import tpu as pltpu
from jax.sharding import PartitionSpec as P

LANES = 128
GROUP = LANES // 2


def signed(modes):
    index = np.arange(modes)
    return np.where(index < modes // 2, index, index - modes)


class Plan:
    def __init__(self, ranks_x, ranks_y, channels, cx, cy, nz, kxd, kyd, mz):
        self.rx, self.ry = ranks_x, ranks_y
        self.c, self.cx, self.cy, self.nz = channels, cx, cy, nz
        self.kxd, self.kyd, self.mz = kxd, kyd, mz
        self.nx, self.ny = cx * ranks_x, cy * ranks_y
        self.mx, self.my = kxd * ranks_x, kyd * ranks_y
        self.devices = ranks_x * ranks_y
        self.slices = self.devices // channels
        self.mzs = mz // self.slices
        self.half = cx // 2
        self.rows = self.half * cy
        self.owned = kxd * kyd
        assert self.devices == self.slices * channels
        assert nz == LANES and 4 * mz == LANES and channels * mz % LANES == 0

    def z_forward(self):
        z = np.arange(self.nz)[:, None]
        kz = np.arange(self.mz)[None, :]
        angle = 2.0 * np.pi / self.nz * (z * kz % self.nz)
        table = np.zeros((self.slices, 2, self.nz, LANES), np.float32)
        for s in range(self.slices):
            part = slice(s * self.mzs, (s + 1) * self.mzs)
            for h in range(2):
                at = h * GROUP
                table[s, h, :, at : at + self.mzs] = np.cos(angle)[:, part]
                table[s, h, :, at + self.mz : at + self.mz + self.mzs] = -np.sin(angle)[:, part]
        return table.reshape(self.slices, 2 * self.nz, LANES)

    def z_inverse(self):
        kz = np.arange(self.mz)[:, None]
        z = np.arange(self.nz)[None, :]
        angle = 2.0 * np.pi / self.nz * (z * kz % self.nz)
        scale = 1.0 / math.sqrt(self.mx * self.my * self.mz)
        table = np.zeros((self.slices, 2, LANES, self.nz), np.float32)
        for s in range(self.slices):
            part = slice(s * self.mzs, (s + 1) * self.mzs)
            for h in range(2):
                at = h * GROUP
                table[s, h, at : at + self.mzs] = scale * np.cos(angle)[part]
                table[s, h, at + self.mz : at + self.mz + self.mzs] = -scale * np.sin(angle)[part]
        return table

    def turns(self):
        kx, ky = signed(self.mx), signed(self.my)
        mode_x = kx.reshape(self.rx, 1, self.kxd, 1)
        mode_y = ky.reshape(1, self.ry, 1, self.kyd)
        shape = (self.rx, self.ry, self.kxd, self.kyd)
        mode_x = np.broadcast_to(mode_x, shape).reshape(-1)
        mode_y = np.broadcast_to(mode_y, shape).reshape(-1)
        x = (np.arange(self.rx)[:, None] * self.cx + np.arange(self.half)).reshape(
            self.rx, 1, self.half, 1
        )
        y = np.arange(self.ny).reshape(1, self.ry, 1, self.cy)
        shape = (self.rx, self.ry, self.half, self.cy)
        x = np.broadcast_to(x, shape).reshape(-1)
        y = np.broadcast_to(y, shape).reshape(-1)
        return mode_x, mode_y, x, y

    def angles(self, shift):
        mode_x, mode_y, x, y = self.turns()
        along_x = mode_x[:, None] * (x[None, :] + shift) % self.nx
        along_y = mode_y[:, None] * y[None, :] % self.ny
        return 2.0 * np.pi * (along_x / self.nx + along_y / self.ny)

    def forward(self):
        angle = self.angles(0)
        return np.concatenate([np.cos(angle), np.sin(angle)], axis=0)

    def shift_phase(self):
        mode_x = self.turns()[0]
        angle = 2.0 * np.pi * (mode_x * self.half % self.nx) / self.nx
        scale = 1.0 / math.sqrt(self.nx * self.ny * self.nz)
        sign = np.where(np.arange(LANES) % GROUP < self.mz, 1.0, -1.0)
        cosine = np.cos(angle)[:, None] * np.ones(LANES)
        sine = np.sin(angle)[:, None] * sign
        return (np.stack([cosine, sine]) * scale).astype(np.float32), scale

    def backward(self):
        halves = []
        for h in range(2):
            angle = self.angles(h * self.half).T
            halves.append(np.concatenate([np.cos(angle), np.sin(angle)], axis=1))
        return np.concatenate(halves, axis=0)

    def spread(self):
        per = LANES // self.mz
        table = np.zeros((self.slices, LANES, 2 * LANES), np.float32)
        for s in range(self.slices):
            for q in range(2):
                for k in range(self.mzs):
                    for o in range(per):
                        table[s, q * self.mz + k, q * LANES + o * self.mz + s * self.mzs + k] = 1
        return table

    def pick(self):
        per = LANES // self.mz
        table = np.zeros((per, self.slices, 2 * LANES, LANES), np.float32)
        for o in range(per):
            for s in range(self.slices):
                for q in range(2):
                    for k in range(self.mzs):
                        row = q * LANES + o * self.mz + s * self.mzs + k
                        for h in range(2):
                            table[o, s, row, h * GROUP + q * self.mz + k] = 1
        return table


def dot(a, b):
    return jnp.dot(a, b, preferred_element_type=jnp.float32)


def lanes_of(shape):
    return lax.broadcasted_iota(jnp.int32, shape, len(shape) - 1)


def to_lines(plan, x_ref, f_ref, out_ref):
    half, c, cy = plan.half, plan.c, plan.cy
    x = x_ref[...]
    low = x[:, :half].reshape(c * plan.rows, LANES)
    high = x[:, half:].reshape(c * plan.rows, LANES)
    cells = jnp.concatenate([low, high], axis=1)
    for s in range(plan.slices):
        line = dot(cells, f_ref[s]).astype(jnp.bfloat16)
        out_ref[:, s] = line.reshape(c, plan.rows, LANES)


def to_modes(plan, x_ref, t_ref, phase_ref, out_ref):
    modes = plan.devices * plan.owned
    x = x_ref[...].reshape(plan.devices * plan.rows, LANES)
    turned = dot(t_ref[...], x)
    cosine, sine = turned[:modes], turned[modes:]
    real = lanes_of((modes, LANES)) % GROUP < plan.mz
    up = LANES - plan.mz
    u = cosine + jnp.where(real, pltpu.roll(sine, up, 1), -pltpu.roll(sine, plan.mz, 1))
    other = jnp.where(real, pltpu.roll(u, plan.mz, 1), pltpu.roll(u, up, 1))
    scale = plan.shift_phase()[1]
    whole = u * scale + phase_ref[0] * pltpu.roll(u, GROUP, 1) + phase_ref[1] * other
    out_ref[...] = whole.reshape(plan.devices, plan.owned, LANES).astype(jnp.bfloat16)


def mix(plan, u_ref, w_ref, spread_ref, pick_ref, out_ref, wide, sums):
    c, owned = plan.c, plan.owned
    blocks = c * plan.mz // LANES
    per = LANES // plan.mz
    u = u_ref[...]
    total = None
    for s in range(plan.slices):
        part = dot(u[:, s].reshape(c * owned, LANES), spread_ref[s])
        total = part if total is None else total + part
    wide[0] = total[:, :LANES]
    wide[1] = total[:, LANES:]
    for m in range(owned):
        u_real = wide[0, pl.ds(m, c, stride=owned), :]
        u_imag = wide[1, pl.ds(m, c, stride=owned), :]
        for j in range(blocks):
            at = pl.ds(j * LANES, LANES)
            w_real = w_ref[m, 0, :, at].astype(jnp.float32)
            w_imag = w_ref[m, 1, :, at].astype(jnp.float32)
            y_real = jnp.sum(w_real * u_real - w_imag * u_imag, axis=0, keepdims=True)
            y_imag = jnp.sum(w_real * u_imag + w_imag * u_real, axis=0, keepdims=True)
            sums[pl.ds(j * owned + m, 1), :LANES] = y_real
            sums[pl.ds(j * owned + m, 1), LANES:] = y_imag
    mixed = sums[...].astype(jnp.bfloat16)
    for o in range(per):
        for s in range(plan.slices):
            line = dot(mixed, pick_ref[o, s]).reshape(blocks, owned, LANES)
            out_ref[:, o, s] = line.astype(jnp.bfloat16)


def from_modes(plan, m_ref, t_ref, out_ref):
    modes = plan.devices * plan.owned
    cells = plan.devices * plan.rows
    m = m_ref[...].reshape(modes, LANES)
    real = lanes_of((modes, LANES)) % GROUP < plan.mz
    swapped = pltpu.roll(m.astype(jnp.float32), plan.mz, 1)
    swapped = jnp.where(real, -swapped, swapped).astype(jnp.bfloat16)
    both = jnp.concatenate([m, swapped], axis=0)
    turned = dot(t_ref[...], both)
    first = lanes_of((cells, LANES)) < GROUP
    out = jnp.where(first, turned[:cells], turned[cells:])
    out_ref[...] = out.reshape(plan.devices, plan.rows, LANES).astype(jnp.bfloat16)


def local_terms(plan, x_ref, d_ref, p_ref, o_ref, out_ref):
    c, cy = plan.c, plan.cy
    size = c * cy
    row = lax.broadcasted_iota(jnp.int32, (size, c), 0) // cy
    pick = (row == lax.broadcasted_iota(jnp.int32, (size, c), 1)).astype(jnp.bfloat16)
    spread = dot(pick, p_ref[...]).astype(jnp.bfloat16)
    wide = lax.dot_general(spread, pick, (((1,), (1,)), ((), ())), preferred_element_type=jnp.float32)
    same = (
        lax.broadcasted_iota(jnp.int32, (size, size), 0) % cy
        == lax.broadcasted_iota(jnp.int32, (size, size), 1) % cy
    )
    mixer = jnp.where(same, wide, 0.0).astype(jnp.bfloat16)
    lane = lanes_of((size, LANES))
    for x in range(plan.cx):
        v = x_ref[:, x].reshape(size, LANES)
        mixing = dot(mixer, v)
        f = v.astype(jnp.float32)
        before = jnp.where(lane == 0, 0.0, pltpu.roll(f, 1, 1))
        after = jnp.where(lane == LANES - 1, 0.0, pltpu.roll(f, LANES - 1, 1))
        curvature = (before + after - 2.0 * f).reshape(c, cy, LANES)
        d = d_ref[x].astype(jnp.float32)
        out_ref[:, x] = mixing.reshape(c, cy, LANES) + d[None] * curvature + o_ref[...]


def finish(plan, s_ref, b_ref, z_ref, out_ref):
    c, half = plan.c, plan.half
    for h in range(2):
        total = None
        for s in range(plan.slices):
            part = dot(s_ref[:, s].reshape(c * plan.rows, LANES), z_ref[s, h])
            total = part if total is None else total + part
        v = total.reshape(c, half, plan.cy, LANES) + b_ref[:, h * half : (h + 1) * half]
        gelu = 0.5 * v * (1.0 + lax.erf(v * math.sqrt(0.5)))
        out_ref[:, h * half : (h + 1) * half] = gelu.astype(jnp.bfloat16)


def call(n, body, plan, out, scratch=(), flops=0, moved=0):
    return pl.pallas_call(
        functools.partial(body, plan),
        out_shape=out,
        in_specs=[pl.BlockSpec(memory_space=pltpu.VMEM)] * n,
        out_specs=pl.BlockSpec(memory_space=pltpu.VMEM),
        compiler_params=pltpu.CompilerParams(vmem_limit_bytes=16 * 2**20),
        scratch_shapes=list(scratch),
        cost_estimate=pl.CostEstimate(flops=flops, bytes_accessed=moved, transcendentals=0),
    )


def on_device(inputs, diffusion, spectral, pointwise, offsets):
    ranks_x = lax.axis_size("gx")
    ranks_y = lax.axis_size("gy")
    c, cx, cy, nz = inputs.shape
    kxd, kyd = spectral.shape[:2]
    plan = Plan(ranks_x, ranks_y, c, cx, cy, nz, kxd, kyd, spectral.shape[4] // c)
    axes = ("gx", "gy")
    bf16 = jnp.bfloat16
    d, s = plan.devices, plan.slices
    shape = jax.ShapeDtypeStruct
    exchange = functools.partial(lax.all_to_all, axis_name=axes, split_axis=0, concat_axis=0, tiled=True)

    def table(values):
        return jnp.asarray(np.asarray(values, np.float32).astype(bf16))

    lines = call(2, to_lines, plan, shape((c, s, plan.rows, LANES), bf16))(
        inputs, table(plan.z_forward())
    )
    lines = exchange(lines.reshape(d, plan.rows, LANES))
    base = call(
        4, local_terms, plan, shape((c, cx, cy, nz), jnp.float32), flops=10**9, moved=10**6
    )(inputs, diffusion, pointwise, jnp.broadcast_to(offsets[:, None, None], (c, cy, LANES)))
    phase = plan.shift_phase()[0]
    modes = call(3, to_modes, plan, shape((d, plan.owned, LANES), bf16))(
        lines, table(plan.forward()), jnp.asarray(phase)
    )
    modes = exchange(modes)
    mixed = call(
        4,
        mix,
        plan,
        shape((c * plan.mz // LANES, LANES // plan.mz, s, plan.owned, LANES), bf16),
        scratch=[
            pltpu.VMEM((2, c * plan.owned, LANES), jnp.float32),
            pltpu.VMEM((c * plan.mz // LANES * plan.owned, 2 * LANES), jnp.float32),
        ],
    )(
        modes.reshape(c, s, plan.owned, LANES),
        spectral.reshape(plan.owned, 2, c, c * plan.mz),
        table(plan.spread()),
        table(plan.pick()),
    )
    mixed = exchange(mixed.reshape(d, plan.owned, LANES))
    spatial = call(2, from_modes, plan, shape((d, plan.rows, LANES), bf16))(
        mixed, table(plan.backward())
    )
    spatial = exchange(spatial)
    return call(3, finish, plan, shape((c, cx, cy, nz), bf16))(
        spatial.reshape(c, s, plan.rows, LANES), base, table(plan.z_inverse())
    )


def solution(mesh):
    in_specs = (
        P(None, "gx", "gy", None),
        P("gx", "gy", None),
        P("gx", "gy", None, None, None),
        P(),
        P(),
    )
    out_specs = P(None, "gx", "gy", None)
    return jax.shard_map(
        on_device, mesh=mesh, in_specs=in_specs, out_specs=out_specs, check_vma=False
    )
```

```python
import functools
import math

import jax
import jax.numpy as jnp
import numpy as np
from jax import lax
from jax.experimental import pallas as pl
from jax.experimental.pallas import tpu as pltpu
from jax.sharding import PartitionSpec as P

LANES = 128
GROUP = LANES // 2


def signed(modes):
    index = np.arange(modes)
    return np.where(index < modes // 2, index, index - modes)


class Plan:
    def __init__(self, ranks_x, ranks_y, channels, cx, cy, nz, kxd, kyd, mz):
        self.rx, self.ry = ranks_x, ranks_y
        self.c, self.cx, self.cy, self.nz = channels, cx, cy, nz
        self.kxd, self.kyd, self.mz = kxd, kyd, mz
        self.nx, self.ny = cx * ranks_x, cy * ranks_y
        self.mx, self.my = kxd * ranks_x, kyd * ranks_y
        self.devices = ranks_x * ranks_y
        self.slices = self.devices // channels
        self.mzs = mz // self.slices
        self.half = cx // 2
        self.rows = self.half * cy
        self.owned = kxd * kyd
        assert self.devices == self.slices * channels
        assert nz == LANES and 4 * mz == LANES and channels * mz % LANES == 0

    def z_forward(self):
        shape = (self.slices, 2 * self.nz, LANES)
        part, row, lane = [lax.broadcasted_iota(jnp.int32, shape, i) for i in range(3)]
        spot = lane % GROUP
        kz = part * self.mzs + spot % self.mz
        angle = 2.0 * math.pi / self.nz * (row * kz % self.nz).astype(jnp.float32)
        used = (row // self.nz == lane // GROUP) & (spot % self.mz < self.mzs)
        value = jnp.where(spot < self.mz, jnp.cos(angle), -jnp.sin(angle))
        return jnp.where(used, value, 0.0).astype(jnp.bfloat16)

    def z_inverse(self):
        kz = np.arange(self.mz)[:, None]
        z = np.arange(self.nz)[None, :]
        angle = 2.0 * np.pi / self.nz * (z * kz % self.nz)
        scale = 1.0 / math.sqrt(self.mx * self.my * self.mz)
        table = np.zeros((self.slices, 2, LANES, self.nz), np.float32)
        for s in range(self.slices):
            part = slice(s * self.mzs, (s + 1) * self.mzs)
            for h in range(2):
                at = h * GROUP
                table[s, h, at : at + self.mzs] = scale * np.cos(angle)[part]
                table[s, h, at + self.mz : at + self.mz + self.mzs] = -scale * np.sin(angle)[part]
        return table

    def turns(self):
        kx, ky = signed(self.mx), signed(self.my)
        mode_x = kx.reshape(self.rx, 1, self.kxd, 1)
        mode_y = ky.reshape(1, self.ry, 1, self.kyd)
        shape = (self.rx, self.ry, self.kxd, self.kyd)
        mode_x = np.broadcast_to(mode_x, shape).reshape(-1)
        mode_y = np.broadcast_to(mode_y, shape).reshape(-1)
        x = (np.arange(self.rx)[:, None] * self.cx + np.arange(self.half)).reshape(
            self.rx, 1, self.half, 1
        )
        y = np.arange(self.ny).reshape(1, self.ry, 1, self.cy)
        shape = (self.rx, self.ry, self.half, self.cy)
        x = np.broadcast_to(x, shape).reshape(-1)
        y = np.broadcast_to(y, shape).reshape(-1)
        return mode_x, mode_y, x, y

    def angles(self, shift):
        mode_x, mode_y, x, y = self.turns()
        along_x = mode_x[:, None] * (x[None, :] + shift) % self.nx
        along_y = mode_y[:, None] * y[None, :] % self.ny
        return 2.0 * np.pi * (along_x / self.nx + along_y / self.ny)

    def forward(self):
        angle = self.angles(0)
        return np.concatenate([np.cos(angle), np.sin(angle)], axis=0)

    def shift_phase(self):
        shape = (self.devices * self.owned, LANES)
        row, lane = [lax.broadcasted_iota(jnp.int32, shape, i) for i in range(2)]
        kx = row // (self.ry * self.owned) * self.kxd + row % self.owned // self.kyd
        kx = jnp.where(kx < self.mx // 2, kx, kx - self.mx)
        angle = 2.0 * math.pi / self.nx * (kx * self.half % self.nx).astype(jnp.float32)
        scale = 1.0 / math.sqrt(self.nx * self.ny * self.nz)
        sine = jnp.sin(angle)
        sine = jnp.where(lane % GROUP < self.mz, sine, -sine)
        return jnp.concatenate([jnp.cos(angle), sine], axis=0) * scale

    def backward(self):
        halves = []
        for h in range(2):
            angle = self.angles(h * self.half).T
            halves.append(np.concatenate([np.cos(angle), np.sin(angle)], axis=1))
        return np.concatenate(halves, axis=0)

    def spread(self):
        per = LANES // self.mz
        table = np.zeros((self.slices, 2, LANES, LANES), np.float32)
        for s in range(self.slices):
            for q in range(2):
                for k in range(self.mzs):
                    for o in range(per):
                        table[s, q, q * self.mz + k, o * self.mz + s * self.mzs + k] = 1
        return table.reshape(-1, LANES)

    def pick(self):
        per = LANES // self.mz
        table = np.zeros((per, self.slices, 2 * LANES, LANES), np.float32)
        for o in range(per):
            for s in range(self.slices):
                for q in range(2):
                    for k in range(self.mzs):
                        row = q * LANES + o * self.mz + s * self.mzs + k
                        for h in range(2):
                            table[o, s, row, h * GROUP + q * self.mz + k] = 1
        return table.reshape(-1, LANES)


def dot(a, b):
    return jnp.dot(a, b, preferred_element_type=jnp.float32)


def lanes_of(shape):
    return lax.broadcasted_iota(jnp.int32, shape, len(shape) - 1)


def to_lines(plan, x_ref, f_ref, out_ref):
    half, c = plan.half, plan.c
    x = x_ref[...]
    low = x[:, :half].reshape(c * plan.rows, LANES)
    high = x[:, half:].reshape(c * plan.rows, LANES)
    cells = jnp.concatenate([low, high], axis=1)
    for s in range(plan.slices):
        line = dot(cells, f_ref[s]).astype(jnp.bfloat16)
        out_ref[:, s] = line.reshape(c, plan.rows, LANES)


def to_modes(plan, x_ref, t_ref, phase_ref, out_ref):
    modes = plan.devices * plan.owned
    x = x_ref[...].reshape(plan.devices * plan.rows, LANES)
    turned = dot(t_ref[...], x)
    cosine, sine = turned[:modes], turned[modes:]
    real = lanes_of((modes, LANES)) % GROUP < plan.mz
    up = LANES - plan.mz
    u = cosine + jnp.where(real, pltpu.roll(sine, up, 1), -pltpu.roll(sine, plan.mz, 1))
    other = jnp.where(real, pltpu.roll(u, plan.mz, 1), pltpu.roll(u, up, 1))
    scale = 1.0 / math.sqrt(plan.nx * plan.ny * plan.nz)
    whole = u * scale + phase_ref[:modes] * pltpu.roll(u, GROUP, 1) + phase_ref[modes:] * other
    out_ref[...] = whole.reshape(plan.devices, plan.owned, LANES).astype(jnp.bfloat16)


def mix(plan, u_ref, w_ref, t_ref, out_ref, wide, sums):
    c, owned = plan.c, plan.owned
    spread_rows = 2 * plan.slices * LANES
    blocks = c * plan.mz // LANES
    per = LANES // plan.mz
    u = u_ref[...]
    total = None
    for s in range(plan.slices):
        part = [
            dot(u[:, s].reshape(c * owned, LANES), t_ref[(2 * s + q) * LANES : (2 * s + q + 1) * LANES])
            for q in range(2)
        ]
        total = part if total is None else [a + b for a, b in zip(total, part)]
    wide[0] = total[0]
    wide[1] = total[1]
    for m in range(owned):
        u_real = wide[0, pl.ds(m, c, stride=owned), :]
        u_imag = wide[1, pl.ds(m, c, stride=owned), :]
        for j in range(blocks):
            at = pl.ds(j * LANES, LANES)
            w_real = w_ref[m, 0, :, at].astype(jnp.float32)
            w_imag = w_ref[m, 1, :, at].astype(jnp.float32)
            y_real = jnp.sum(w_real * u_real - w_imag * u_imag, axis=0, keepdims=True)
            y_imag = jnp.sum(w_real * u_imag + w_imag * u_real, axis=0, keepdims=True)
            sums[pl.ds(j * owned + m, 1), :LANES] = y_real
            sums[pl.ds(j * owned + m, 1), LANES:] = y_imag
    mixed = sums[...].astype(jnp.bfloat16)
    for o in range(per):
        for s in range(plan.slices):
            at = spread_rows + (o * plan.slices + s) * 2 * LANES
            line = dot(mixed, t_ref[at : at + 2 * LANES]).reshape(blocks, owned, LANES)
            out_ref[:, o, s] = line.astype(jnp.bfloat16)


def from_modes(plan, m_ref, t_ref, out_ref):
    modes = plan.devices * plan.owned
    cells = plan.devices * plan.rows
    m = m_ref[...].reshape(modes, LANES)
    real = lanes_of((modes, LANES)) % GROUP < plan.mz
    swapped = pltpu.roll(m.astype(jnp.float32), plan.mz, 1)
    swapped = jnp.where(real, -swapped, swapped).astype(jnp.bfloat16)
    both = jnp.concatenate([m, swapped], axis=0)
    turned = dot(t_ref[...], both)
    first = lanes_of((cells, LANES)) < GROUP
    out = jnp.where(first, turned[:cells], turned[cells:])
    out_ref[...] = out.reshape(plan.devices, plan.rows, LANES).astype(jnp.bfloat16)


def local_terms(plan, x_ref, d_ref, p_ref, o_ref, out_ref):
    c, cy = plan.c, plan.cy
    size = c * cy
    row = lax.broadcasted_iota(jnp.int32, (size, c), 0) // cy
    pick = (row == lax.broadcasted_iota(jnp.int32, (size, c), 1)).astype(jnp.bfloat16)
    spread = dot(pick, p_ref[...]).astype(jnp.bfloat16)
    wide = lax.dot_general(spread, pick, (((1,), (1,)), ((), ())), preferred_element_type=jnp.float32)
    same = (
        lax.broadcasted_iota(jnp.int32, (size, size), 0) % cy
        == lax.broadcasted_iota(jnp.int32, (size, size), 1) % cy
    )
    mixer = jnp.where(same, wide, 0.0).astype(jnp.bfloat16)
    lane = lanes_of((size, LANES))
    for x in range(plan.cx):
        v = x_ref[:, x].reshape(size, LANES)
        mixing = dot(mixer, v)
        f = v.astype(jnp.float32)
        before = jnp.where(lane == 0, 0.0, pltpu.roll(f, 1, 1))
        after = jnp.where(lane == LANES - 1, 0.0, pltpu.roll(f, LANES - 1, 1))
        curvature = (before + after - 2.0 * f).reshape(c, cy, LANES)
        d = d_ref[x].astype(jnp.float32)
        out_ref[:, x] = mixing.reshape(c, cy, LANES) + d[None] * curvature + o_ref[...]


def finish(plan, s_ref, b_ref, z_ref, out_ref):
    c, half = plan.c, plan.half
    for h in range(2):
        total = None
        for s in range(plan.slices):
            part = dot(s_ref[:, s].reshape(c * plan.rows, LANES), z_ref[s, h])
            total = part if total is None else total + part
        v = total.reshape(c, half, plan.cy, LANES) + b_ref[:, h * half : (h + 1) * half]
        gelu = 0.5 * v * (1.0 + lax.erf(v * math.sqrt(0.5)))
        out_ref[:, h * half : (h + 1) * half] = gelu.astype(jnp.bfloat16)


def call(n, body, plan, out, scratch=(), flops=0, moved=0):
    return pl.pallas_call(
        functools.partial(body, plan),
        out_shape=out,
        in_specs=[pl.BlockSpec(memory_space=pltpu.VMEM)] * n,
        out_specs=pl.BlockSpec(memory_space=pltpu.VMEM),
        compiler_params=pltpu.CompilerParams(vmem_limit_bytes=16 * 2**20),
        scratch_shapes=list(scratch),
        cost_estimate=pl.CostEstimate(flops=flops, bytes_accessed=moved, transcendentals=0),
    )


def on_device(inputs, diffusion, spectral, pointwise, offsets):
    ranks_x = lax.axis_size("gx")
    ranks_y = lax.axis_size("gy")
    c, cx, cy, nz = inputs.shape
    kxd, kyd = spectral.shape[:2]
    plan = Plan(ranks_x, ranks_y, c, cx, cy, nz, kxd, kyd, spectral.shape[4] // c)
    axes = ("gx", "gy")
    bf16 = jnp.bfloat16
    d, s = plan.devices, plan.slices
    shape = jax.ShapeDtypeStruct
    exchange = functools.partial(lax.all_to_all, axis_name=axes, split_axis=0, concat_axis=0, tiled=True)

    def table(values):
        return jnp.asarray(np.asarray(values, np.float32).astype(bf16))

    lines = call(2, to_lines, plan, shape((c, s, plan.rows, LANES), bf16))(
        inputs, plan.z_forward()
    )
    lines = exchange(lines.reshape(d, plan.rows, LANES))
    base = call(
        4, local_terms, plan, shape((c, cx, cy, nz), jnp.float32), flops=10**9, moved=10**6
    )(inputs, diffusion, pointwise, jnp.broadcast_to(offsets[:, None, None], (c, cy, LANES)))
    modes = call(3, to_modes, plan, shape((d, plan.owned, LANES), bf16))(
        lines, table(plan.forward()), plan.shift_phase()
    )
    modes = exchange(modes)
    mixed = call(
        3,
        mix,
        plan,
        shape((c * plan.mz // LANES, LANES // plan.mz, s, plan.owned, LANES), bf16),
        scratch=[
            pltpu.VMEM((2, c * plan.owned, LANES), jnp.float32),
            pltpu.VMEM((c * plan.mz // LANES * plan.owned, 2 * LANES), jnp.float32),
        ],
    )(
        modes.reshape(c, s, plan.owned, LANES),
        spectral.reshape(plan.owned, 2, c, c * plan.mz),
        table(np.concatenate([plan.spread(), plan.pick()], axis=0)),
    )
    mixed = exchange(mixed.reshape(d, plan.owned, LANES))
    spatial = call(2, from_modes, plan, shape((d, plan.rows, LANES), bf16))(
        mixed, table(plan.backward())
    )
    spatial = exchange(spatial)
    return call(3, finish, plan, shape((c, cx, cy, nz), bf16))(
        spatial.reshape(c, s, plan.rows, LANES), base, table(plan.z_inverse())
    )


def solution(mesh):
    in_specs = (
        P(None, "gx", "gy", None),
        P("gx", "gy", None),
        P("gx", "gy", None, None, None),
        P(),
        P(),
    )
    out_specs = P(None, "gx", "gy", None)
    return jax.shard_map(
        on_device, mesh=mesh, in_specs=in_specs, out_specs=out_specs, check_vma=False
    )
```

```python
import functools
import math

import jax
import jax.numpy as jnp
import numpy as np
from jax import lax
from jax.experimental import pallas as pl
from jax.experimental.pallas import tpu as pltpu
from jax.sharding import PartitionSpec as P

LANES = 128
GROUP = LANES // 2
QUARTER = LANES // 4


class Plan:
    def __init__(self, ranks_x, ranks_y, inputs, spectral):
        self.rx, self.ry = ranks_x, ranks_y
        self.c, self.cx, self.cy, self.nz = inputs.shape
        self.kxd, self.kyd = spectral.shape[:2]
        self.mz = spectral.shape[4] // self.c
        self.nx, self.ny = self.cx * ranks_x, self.cy * ranks_y
        self.mx, self.my = self.kxd * ranks_x, self.kyd * ranks_y
        self.pairs = self.kyd // 2
        self.blocks = self.c * self.mz // LANES
        self.per = LANES // self.mz
        first = ranks_x // 4
        self.order = [first] + [i for i in range(ranks_x) if i != first]
        assert self.nz == LANES and self.mz == QUARTER and self.kyd % 2 == 0
        assert ranks_y & (ranks_y - 1) == 0 and self.blocks == 8 and self.cy == 8


def dot(a, b):
    return jnp.dot(a, b, preferred_element_type=jnp.float32)


def iota(shape, axis):
    return lax.broadcasted_iota(jnp.int32, shape, axis)


def wave(winding, length):
    return jnp.cos(2.0 * math.pi / length * (winding % length).astype(jnp.float32))


def to_partial(plan, x_ref, *refs):
    outs, (spectrum, pieces, waves) = refs[: plan.ry], refs[plan.ry :]
    rows, c, cx, cy, ny = plan.c * plan.cx * plan.cy, plan.c, plan.cx, plan.cy, plan.ny
    mine = lax.axis_index("gy")
    z, lane = iota((LANES, LANES), 0), iota((LANES, LANES), 1)
    turn = (lane // QUARTER + 1) // 2 * (plan.nz // 4)
    forward = wave(z * (lane % QUARTER) + turn, plan.nz).astype(jnp.bfloat16)
    spectrum[...] = dot(x_ref[...].reshape(rows, LANES), forward)
    half = plan.my // 2
    shape = ((half + 1) * cy, LANES)
    row, lane = iota(shape, 0), iota(shape, 1)
    winding = row // cy * (mine * cy + row % cy) - lane // GROUP * (ny // 4)
    waves[...] = wave(winding + ny, ny)
    low = iota((c, LANES), 1) < GROUP
    for x in range(cx):
        planes = [spectrum[pl.ds(x * cy + y, c, stride=cx * cy), :] for y in range(cy)]
        sums = []
        for k in range(half + 1):
            total = None
            for y in range(cy):
                term = waves[pl.ds(k * cy + y, 1), :] * planes[y]
                total = term if total is None else total + term
            sums.append((total, pltpu.roll(total, GROUP, 1)))
        for i in range(plan.my // 2):
            sides = []
            for side, j in enumerate((2 * i, 2 * i + 1)):
                if j < half:
                    a, b = sums[j]
                    sides.append(a + b)
                else:
                    a, b = sums[plan.my - j]
                    sides.append(b - a if side else a - b)
            value = jnp.where(low, sides[0], sides[1]).astype(jnp.bfloat16)
            pieces[i // plan.pairs, i % plan.pairs, x] = value
    for k in range(plan.ry):
        outs[k][...] = pieces[mine ^ k]


def to_modes(plan, *refs):
    parts, (out_ref, waves) = refs[: plan.ry], refs[plan.ry :]
    c, cx, nx = plan.c, plan.cx, plan.nx
    half = plan.mx // 2
    count = (half + 1) * cx
    row = iota((2 * count, LANES), 0)
    place = lax.axis_index("gx") * cx + row % cx
    winding = row // cx % (half + 1) * place - row // count * (nx // 4)
    waves[...] = wave(winding + nx, nx)
    real = iota((c, LANES), 1) % GROUP < QUARTER
    for p in range(plan.pairs):
        lines, turned = [], []
        for x in range(cx):
            line = sum(part[p, x].astype(jnp.float32) for part in parts)
            lines.append(line)
            up, down = pltpu.roll(line, LANES - QUARTER, 1), pltpu.roll(line, QUARTER, 1)
            turned.append(jnp.where(real, up, -down))
        for k in range(half + 1):
            even = odd = None
            for x in range(cx):
                cosine = waves[pl.ds(k * cx + x, 1), :] * lines[x]
                sine = waves[pl.ds(count + k * cx + x, 1), :] * turned[x]
                even = cosine if even is None else even + cosine
                odd = sine if odd is None else odd + sine
            if k < half:
                owner = plan.order.index(k // plan.kxd)
                out_ref[owner, k % plan.kxd, p] = (even + odd).astype(jnp.bfloat16)
            if k > 0:
                back = plan.mx - k
                owner = plan.order.index(back // plan.kxd)
                out_ref[owner, back % plan.kxd, p] = (even - odd).astype(jnp.bfloat16)


def mix(plan, u_ref, w_ref, out_ref, sums):
    c = plan.c
    scale = 1.0 / math.sqrt(plan.nx * plan.ny * plan.nz)
    group = iota((c, LANES), 1) // QUARTER
    for kx in range(plan.kxd):
        for p in range(plan.pairs):
            u = sum(u_ref[r, kx, p].astype(jnp.float32) for r in range(plan.rx)) * scale
            rolled = [u] + [pltpu.roll(u, v * QUARTER, 1) for v in range(1, 4)]

            def spread(g):
                value = rolled[(3 - g) % 4]
                for j in (2, 1, 0):
                    value = jnp.where(group == j, rolled[(j - g) % 4], value)
                return value

            for side in range(2):
                ky = 2 * p + side
                u_real, u_imag = spread(2 * side), spread(2 * side + 1)
                for j in range(plan.blocks):
                    at = pl.ds(j * LANES, LANES)
                    w_real = w_ref[kx, ky, 0, :, at].astype(jnp.float32)
                    w_imag = w_ref[kx, ky, 1, :, at].astype(jnp.float32)
                    y_real = jnp.sum(w_real * u_real - w_imag * u_imag, axis=0, keepdims=True)
                    y_imag = jnp.sum(w_real * u_imag + w_imag * u_real, axis=0, keepdims=True)
                    sums[ky, kx, 0, pl.ds(j, 1), :] = y_real
                    sums[ky, kx, 1, pl.ds(j, 1), :] = y_imag
    mixed = sums[...].astype(jnp.bfloat16)
    for r in range(plan.rx):
        out_ref[r] = mixed


def from_kx(plan, m_ref, t_ref, out_ref):
    depth = plan.rx * plan.kxd * 2 * plan.blocks
    for ky in range(plan.kyd):
        lines = dot(t_ref[...], m_ref[:, ky].reshape(depth, LANES))
        lines = lines.reshape(plan.cx, 2, plan.blocks, LANES)
        out_ref[:, ky] = lines.astype(jnp.bfloat16)


def local_terms(plan, x_ref, d_ref, p_ref, o_ref, out_ref):
    c, cy = plan.c, plan.cy
    size = c * cy
    row = iota((size, c), 0) // cy
    pick = (row == iota((size, c), 1)).astype(jnp.bfloat16)
    spread = dot(pick, p_ref[...]).astype(jnp.bfloat16)
    wide = lax.dot_general(
        spread, pick, (((1,), (1,)), ((), ())), preferred_element_type=jnp.float32
    )
    same = iota((size, size), 0) % cy == iota((size, size), 1) % cy
    mixer = jnp.where(same, wide, 0.0).astype(jnp.bfloat16)
    lane = iota((size, LANES), 1)
    for x in range(plan.cx):
        v = x_ref[:, x].reshape(size, LANES)
        mixing = dot(mixer, v)
        f = v.astype(jnp.float32)
        before = jnp.where(lane == 0, 0.0, pltpu.roll(f, 1, 1))
        after = jnp.where(lane == LANES - 1, 0.0, pltpu.roll(f, LANES - 1, 1))
        curvature = (before + after - 2.0 * f).reshape(c, cy, LANES)
        d = d_ref[x].astype(jnp.float32)
        out_ref[:, x] = mixing.reshape(c, cy, LANES) + d[None] * curvature + o_ref[...]


def finish(plan, *refs):
    parts, (b_ref, y_ref, z_ref, out_ref) = refs[: plan.ry], refs[plan.ry :]
    size = plan.kyd * 2 * plan.blocks
    half = plan.blocks * plan.cy
    for x in range(plan.cx):
        held = jnp.concatenate([part[x].reshape(size, LANES) for part in parts], axis=0)
        lines = dot(y_ref[...], held).astype(jnp.bfloat16)
        lines = jnp.concatenate([lines[:half], lines[half:]], axis=1)
        spectral = dot(lines, z_ref[...])
        for o in range(plan.per):
            v = spectral[:, o * LANES : (o + 1) * LANES].reshape(plan.blocks, plan.cy, LANES)
            v = v + b_ref[:, o, x]
            gelu = 0.5 * v * (1.0 + lax.erf(v * math.sqrt(0.5)))
            out_ref[:, o, x] = gelu.astype(jnp.bfloat16)


def x_table(plan):
    b = plan.blocks
    shape = (plan.cx * 2 * b, plan.rx * plan.kxd * 2 * b)
    row, column = iota(shape, 0), iota(shape, 1)
    order = jnp.asarray(plan.order, jnp.int32)[jnp.arange(shape[1]) // (plan.kxd * 2 * b)]
    kx = order[None, :] * plan.kxd + column // (2 * b) % plan.kxd
    kx = jnp.where(kx < plan.mx // 2, kx, kx - plan.mx)
    x = lax.axis_index("gx") * plan.cx + row // (2 * b)
    turn = (column // b % 2 - row // b % 2) * (plan.nx // 4)
    winding = kx * x + turn + plan.nx * plan.nx
    return jnp.where(row % b == column % b, wave(winding, plan.nx), 0.0).astype(jnp.bfloat16)


def y_table(plan):
    b, cy = plan.blocks, plan.cy
    shape = (2 * b * cy, plan.ry * plan.kyd * 2 * b)
    row, column = iota(shape, 0), iota(shape, 1)
    rank = column // (plan.kyd * 2 * b) ^ lax.axis_index("gy")
    ky = rank * plan.kyd + column // (2 * b) % plan.kyd
    ky = jnp.where(ky < plan.my // 2, ky, ky - plan.my)
    y = lax.axis_index("gy") * cy + row % cy
    turn = (column // b % 2 - row // (b * cy)) * (plan.ny // 4)
    winding = ky * y + turn + plan.ny * plan.ny
    return jnp.where(row // cy % b == column % b, wave(winding, plan.ny), 0.0).astype(jnp.bfloat16)


def z_table(plan):
    row = np.arange(2 * LANES)[:, None]
    column = np.arange(plan.per * LANES)[None, :]
    angle = 2.0 * np.pi / plan.nz * (row % plan.mz * column % plan.nz)
    value = np.where(row < LANES, np.cos(angle), -np.sin(angle))
    value = value / math.sqrt(plan.mx * plan.my * plan.mz)
    value = np.where(row % LANES // plan.mz == column // LANES, value, 0.0)
    return jnp.asarray(value.astype(np.float32).astype(jnp.bfloat16))


def call(n, body, plan, out, scratch=(), flops=0, moved=0):
    vmem = pl.BlockSpec(memory_space=pltpu.VMEM)
    return pl.pallas_call(
        functools.partial(body, plan),
        out_shape=out,
        in_specs=[vmem] * n,
        out_specs=jax.tree.map(lambda _: vmem, out),
        compiler_params=pltpu.CompilerParams(vmem_limit_bytes=16 * 2**20),
        scratch_shapes=list(scratch),
        cost_estimate=pl.CostEstimate(flops=flops, bytes_accessed=moved, transcendentals=0),
    )


def on_device(inputs, diffusion, spectral, pointwise, offsets):
    plan = Plan(lax.axis_size("gx"), lax.axis_size("gy"), inputs, spectral)
    c, cx, cy, nz = inputs.shape
    rx, ry, kxd, kyd, b = plan.rx, plan.ry, plan.kxd, plan.kyd, plan.blocks
    bf16, f32 = jnp.bfloat16, jnp.float32
    shape = jax.ShapeDtypeStruct
    order = [plan.order]

    def swap(value, k):
        return lax.ppermute(value, "gy", [(i, i ^ k) for i in range(ry)]) if k else value

    def exchange(value):
        return lax.all_to_all(
            value, "gx", split_axis=0, concat_axis=0, axis_index_groups=order, tiled=True
        )

    partial = call(
        1,
        to_partial,
        plan,
        [shape((plan.pairs, cx, c, LANES), bf16)] * ry,
        scratch=[
            pltpu.VMEM((c * cx * cy, LANES), f32),
            pltpu.VMEM((ry, plan.pairs, cx, c, LANES), bf16),
            pltpu.VMEM(((plan.my // 2 + 1) * cy, LANES), f32),
        ],
    )(inputs)
    lines = [swap(partial[k], k) for k in range(ry)]
    base = call(4, local_terms, plan, shape((c, cx, cy, nz), f32), flops=10**9, moved=10**6)(
        inputs, diffusion, pointwise, jnp.broadcast_to(offsets[:, None, None], (c, cy, LANES))
    )
    modes = call(
        ry,
        to_modes,
        plan,
        shape((rx, kxd, plan.pairs, c, LANES), bf16),
        scratch=[pltpu.VMEM((2 * (plan.mx // 2 + 1) * cx, LANES), f32)],
    )(*lines)
    modes = exchange(modes)
    mixed = call(
        2,
        mix,
        plan,
        shape((rx, kyd, kxd, 2, b, LANES), bf16),
        scratch=[pltpu.VMEM((kyd, kxd, 2, b, LANES), f32)],
    )(modes, spectral)
    mixed = exchange(mixed)
    held = call(2, from_kx, plan, shape((cx, kyd, 2, b, LANES), bf16))(mixed, x_table(plan))
    parts = [swap(held, k) for k in range(ry)]
    out = call(ry + 3, finish, plan, shape((b, plan.per, cx, cy, nz), bf16))(
        *parts, base.reshape(b, plan.per, cx, cy, nz), y_table(plan), z_table(plan)
    )
    return out.reshape(c, cx, cy, nz)


def solution(mesh):
    in_specs = (
        P(None, "gx", "gy", None),
        P("gx", "gy", None),
        P("gx", "gy", None, None, None),
        P(),
        P(),
    )
    out_specs = P(None, "gx", "gy", None)
    return jax.shard_map(
        on_device, mesh=mesh, in_specs=in_specs, out_specs=out_specs, check_vma=False
    )
```

```python
import functools
import math

import jax
import jax.numpy as jnp
import numpy as np
from jax import lax
from jax.experimental import pallas as pl
from jax.experimental.pallas import tpu as pltpu
from jax.sharding import PartitionSpec as P

LANES = 128
GROUP = LANES // 2
QUARTER = LANES // 4


class Plan:
    def __init__(self, ranks_x, ranks_y, inputs, spectral):
        self.rx, self.ry = ranks_x, ranks_y
        self.c, self.cx, self.cy, self.nz = inputs.shape
        self.kxd, self.kyd = spectral.shape[:2]
        self.mz = spectral.shape[4] // self.c
        self.nx, self.ny = self.cx * ranks_x, self.cy * ranks_y
        self.mx, self.my = self.kxd * ranks_x, self.kyd * ranks_y
        self.pairs = self.kyd // 2
        self.blocks = self.c * self.mz // LANES
        self.per = LANES // self.mz
        first = ranks_x // 4
        self.order = [first] + [i for i in range(ranks_x) if i != first]
        assert self.nz == LANES and self.mz == QUARTER and self.kyd % 2 == 0
        assert ranks_y & (ranks_y - 1) == 0 and self.blocks == 8 and self.cy == 8


def dot(a, b):
    return jnp.dot(a, b, preferred_element_type=jnp.float32)


def iota(shape, axis):
    return lax.broadcasted_iota(jnp.int32, shape, axis)


def wave(winding, length):
    return jnp.cos(2.0 * math.pi / length * (winding % length).astype(jnp.float32))


def prepare(plan, waves_ref, forward_ref, regroup_ref):
    cy, ny, size = plan.cy, plan.ny, plan.c * plan.cy
    mine = lax.axis_index("gy")
    row, lane = iota(waves_ref.shape, 0), iota(waves_ref.shape, 1)
    winding = row // cy * (mine * cy + row % cy) - lane // GROUP * (ny // 4)
    waves_ref[...] = wave(winding + ny, ny)
    z, lane = iota((LANES, LANES), 0), iota((LANES, LANES), 1)
    turn = (lane // QUARTER + 1) // 2 * (plan.nz // 4)
    forward_ref[...] = wave(z * (lane % QUARTER) + turn, plan.nz).astype(jnp.bfloat16)
    row, column = iota((size, size), 0), iota((size, size), 1)
    same = row % plan.c * cy + row // plan.c == column
    regroup_ref[...] = same.astype(jnp.float32).astype(jnp.bfloat16)


def to_partial(plan, x_ref, waves, forward_ref, regroup_ref, *refs):
    outs, (pieces,) = refs[: plan.ry], refs[plan.ry :]
    c, cx, cy = plan.c, plan.cx, plan.cy
    size, half = c * cy, plan.my // 2
    mine = lax.axis_index("gy")
    forward, regroup = forward_ref[...], regroup_ref[...]
    low = iota((c // 2, LANES), 1) < GROUP
    for x in range(0, cx, 2):
        pair = [x_ref[:, x + i].reshape(size, LANES) for i in range(2)]
        pair = dot(regroup, jnp.concatenate(pair, axis=1)).astype(jnp.bfloat16)
        for i in range(2):
            spectrum = dot(pair[:, i * LANES : (i + 1) * LANES], forward)
            for part in range(2):
                begin = part * (c // 2)
                planes = [spectrum[y * c + begin : y * c + begin + c // 2] for y in range(cy)]
                sums = []
                for k in range(half + 1):
                    total = None
                    for y in range(cy):
                        term = waves[pl.ds(k * cy + y, 1), :] * planes[y]
                        total = term if total is None else total + term
                    sums.append((total, pltpu.roll(total, GROUP, 1)))
                for t in range(plan.my // 2):
                    sides = []
                    for side, j in enumerate((2 * t, 2 * t + 1)):
                        if j < half:
                            a, b = sums[j]
                            sides.append(a + b)
                        else:
                            a, b = sums[plan.my - j]
                            sides.append(b - a if side else a - b)
                    value = jnp.where(low, sides[0], sides[1]).astype(jnp.bfloat16)
                    pieces[t // plan.pairs, t % plan.pairs, x + i, pl.ds(begin, c // 2)] = value
    for k in range(plan.ry):
        outs[k][...] = pieces[mine ^ k]


def to_modes(plan, *refs):
    parts, (out_ref, waves) = refs[: plan.ry], refs[plan.ry :]
    c, cx, nx = plan.c, plan.cx, plan.nx
    half = plan.mx // 2
    count = (half + 1) * cx
    row = iota((2 * count, LANES), 0)
    place = lax.axis_index("gx") * cx + row % cx
    winding = row // cx % (half + 1) * place - row // count * (nx // 4)
    waves[...] = wave(winding + nx, nx)
    real = iota((c, LANES), 1) % GROUP < QUARTER
    for p in range(plan.pairs):
        lines, turned = [], []
        for x in range(cx):
            line = sum(part[p, x].astype(jnp.float32) for part in parts)
            lines.append(line)
            up, down = pltpu.roll(line, LANES - QUARTER, 1), pltpu.roll(line, QUARTER, 1)
            turned.append(jnp.where(real, up, -down))
        for k in range(half + 1):
            even = odd = None
            for x in range(cx):
                cosine = waves[pl.ds(k * cx + x, 1), :] * lines[x]
                sine = waves[pl.ds(count + k * cx + x, 1), :] * turned[x]
                even = cosine if even is None else even + cosine
                odd = sine if odd is None else odd + sine
            if k < half:
                owner = plan.order.index(k // plan.kxd)
                out_ref[owner, k % plan.kxd, p] = (even + odd).astype(jnp.bfloat16)
            if k > 0:
                back = plan.mx - k
                owner = plan.order.index(back // plan.kxd)
                out_ref[owner, back % plan.kxd, p] = (even - odd).astype(jnp.bfloat16)


def mix(plan, u_ref, w_ref, out_ref, sums):
    c = plan.c
    scale = 1.0 / math.sqrt(plan.nx * plan.ny * plan.nz)
    group = iota((c, LANES), 1) // QUARTER
    for kx in range(plan.kxd):
        for p in range(plan.pairs):
            u = sum(u_ref[r, kx, p].astype(jnp.float32) for r in range(plan.rx)) * scale
            rolled = [u] + [pltpu.roll(u, v * QUARTER, 1) for v in range(1, 4)]

            def spread(g):
                value = rolled[(3 - g) % 4]
                for j in (2, 1, 0):
                    value = jnp.where(group == j, rolled[(j - g) % 4], value)
                return value

            for side in range(2):
                ky = 2 * p + side
                u_real, u_imag = spread(2 * side), spread(2 * side + 1)
                for j in range(plan.blocks):
                    at = pl.ds(j * LANES, LANES)
                    w_real = w_ref[kx, ky, 0, :, at].astype(jnp.float32)
                    w_imag = w_ref[kx, ky, 1, :, at].astype(jnp.float32)
                    y_real = jnp.sum(w_real * u_real - w_imag * u_imag, axis=0, keepdims=True)
                    y_imag = jnp.sum(w_real * u_imag + w_imag * u_real, axis=0, keepdims=True)
                    sums[ky, kx, 0, pl.ds(j, 1), :] = y_real
                    sums[ky, kx, 1, pl.ds(j, 1), :] = y_imag
    mixed = sums[...].astype(jnp.bfloat16)
    for r in range(plan.rx):
        out_ref[r] = mixed


def from_kx(plan, m_ref, t_ref, out_ref):
    depth = plan.rx * plan.kxd * 2 * plan.blocks
    for ky in range(plan.kyd):
        lines = dot(t_ref[...], m_ref[:, ky].reshape(depth, LANES))
        lines = lines.reshape(plan.cx, 2, plan.blocks, LANES)
        out_ref[:, ky] = lines.astype(jnp.bfloat16)


def local_terms(plan, x_ref, d_ref, p_ref, o_ref, out_ref):
    c, cy = plan.c, plan.cy
    size = c * cy
    row = iota((size, c), 0) // cy
    pick = (row == iota((size, c), 1)).astype(jnp.bfloat16)
    spread = dot(pick, p_ref[...]).astype(jnp.bfloat16)
    wide = lax.dot_general(
        spread, pick, (((1,), (1,)), ((), ())), preferred_element_type=jnp.float32
    )
    same = iota((size, size), 0) % cy == iota((size, size), 1) % cy
    mixer = jnp.where(same, wide, 0.0).astype(jnp.bfloat16)
    lane = iota((size, LANES), 1)
    for x in range(plan.cx):
        v = x_ref[:, x].reshape(size, LANES)
        mixing = dot(mixer, v)
        f = v.astype(jnp.float32)
        before = jnp.where(lane == 0, 0.0, pltpu.roll(f, 1, 1))
        after = jnp.where(lane == LANES - 1, 0.0, pltpu.roll(f, LANES - 1, 1))
        curvature = (before + after - 2.0 * f).reshape(c, cy, LANES)
        d = d_ref[x].astype(jnp.float32)
        out_ref[:, x] = mixing.reshape(c, cy, LANES) + d[None] * curvature + o_ref[...]


def finish(plan, *refs):
    parts, (b_ref, y_ref, z_ref, out_hbm, held_out, sems) = refs[: plan.ry], refs[plan.ry :]
    size = plan.kyd * 2 * plan.blocks
    half = plan.blocks * plan.cy
    copies = []
    for x in range(plan.cx):
        held = jnp.concatenate([part[x].reshape(size, LANES) for part in parts], axis=0)
        lines = dot(y_ref[...], held).astype(jnp.bfloat16)
        lines = jnp.concatenate([lines[:half], lines[half:]], axis=1)
        spectral = dot(lines, z_ref[...])
        for o in range(plan.per):
            v = spectral[:, o * LANES : (o + 1) * LANES].reshape(plan.blocks, plan.cy, LANES)
            v = v + b_ref[:, o, x]
            gelu = 0.5 * v * (1.0 + lax.erf(v * math.sqrt(0.5)))
            held_out[x, :, o] = gelu.astype(jnp.bfloat16)
        copies.append(pltpu.make_async_copy(held_out.at[x], out_hbm.at[:, :, x], sems.at[x]))
        copies[-1].start()
    for copy in copies:
        copy.wait()


def x_table(plan):
    b = plan.blocks
    shape = (plan.cx * 2 * b, plan.rx * plan.kxd * 2 * b)
    row, column = iota(shape, 0), iota(shape, 1)
    order = jnp.asarray(plan.order, jnp.int32)[jnp.arange(shape[1]) // (plan.kxd * 2 * b)]
    kx = order[None, :] * plan.kxd + column // (2 * b) % plan.kxd
    kx = jnp.where(kx < plan.mx // 2, kx, kx - plan.mx)
    x = lax.axis_index("gx") * plan.cx + row // (2 * b)
    turn = (column // b % 2 - row // b % 2) * (plan.nx // 4)
    winding = kx * x + turn + plan.nx * plan.nx
    return jnp.where(row % b == column % b, wave(winding, plan.nx), 0.0).astype(jnp.bfloat16)


def y_table(plan):
    b, cy = plan.blocks, plan.cy
    shape = (2 * b * cy, plan.ry * plan.kyd * 2 * b)
    row, column = iota(shape, 0), iota(shape, 1)
    rank = column // (plan.kyd * 2 * b) ^ lax.axis_index("gy")
    ky = rank * plan.kyd + column // (2 * b) % plan.kyd
    ky = jnp.where(ky < plan.my // 2, ky, ky - plan.my)
    y = lax.axis_index("gy") * cy + row % cy
    turn = (column // b % 2 - row // (b * cy)) * (plan.ny // 4)
    winding = ky * y + turn + plan.ny * plan.ny
    return jnp.where(row // cy % b == column % b, wave(winding, plan.ny), 0.0).astype(jnp.bfloat16)


def z_table(plan):
    row = np.arange(2 * LANES)[:, None]
    column = np.arange(plan.per * LANES)[None, :]
    angle = 2.0 * np.pi / plan.nz * (row % plan.mz * column % plan.nz)
    value = np.where(row < LANES, np.cos(angle), -np.sin(angle))
    value = value / math.sqrt(plan.mx * plan.my * plan.mz)
    value = np.where(row % LANES // plan.mz == column // LANES, value, 0.0)
    return jnp.asarray(value.astype(np.float32).astype(jnp.bfloat16))


def call(n, body, plan, out, scratch=(), flops=0, moved=0, outer=(pltpu.VMEM, pltpu.VMEM)):
    near = pl.BlockSpec(memory_space=outer[0])
    vmem = pl.BlockSpec(memory_space=outer[1])
    return pl.pallas_call(
        functools.partial(body, plan),
        out_shape=out,
        in_specs=[near] * n,
        out_specs=jax.tree.map(lambda _: vmem, out),
        compiler_params=pltpu.CompilerParams(vmem_limit_bytes=16 * 2**20),
        scratch_shapes=list(scratch),
        cost_estimate=pl.CostEstimate(flops=flops, bytes_accessed=moved, transcendentals=0),
    )


def on_device(inputs, diffusion, spectral, pointwise, offsets):
    plan = Plan(lax.axis_size("gx"), lax.axis_size("gy"), inputs, spectral)
    c, cx, cy, nz = inputs.shape
    rx, ry, kxd, kyd, b = plan.rx, plan.ry, plan.kxd, plan.kyd, plan.blocks
    bf16, f32 = jnp.bfloat16, jnp.float32
    shape = jax.ShapeDtypeStruct
    order = [plan.order]

    def swap(value, k):
        return lax.ppermute(value, "gy", [(i, i ^ k) for i in range(ry)]) if k else value

    def exchange(value):
        return lax.all_to_all(
            value, "gx", split_axis=0, concat_axis=0, axis_index_groups=order, tiled=True
        )

    size = c * cy
    tables = call(
        0,
        prepare,
        plan,
        [
            shape(((plan.my // 2 + 1) * cy, LANES), f32),
            shape((LANES, LANES), bf16),
            shape((size, size), bf16),
        ],
        flops=10**9,
        moved=4 * 10**6,
    )()
    partial = call(
        4,
        to_partial,
        plan,
        [shape((plan.pairs, cx, c, LANES), bf16)] * ry,
        scratch=[pltpu.VMEM((ry, plan.pairs, cx, c, LANES), bf16)],
    )(inputs, *tables)
    lines = [swap(partial[k], k) for k in range(ry)]
    base = call(4, local_terms, plan, shape((c, cx, cy, nz), f32), flops=10**9, moved=10**6)(
        inputs, diffusion, pointwise, jnp.broadcast_to(offsets[:, None, None], (c, cy, LANES))
    )
    x_inverse, y_inverse = x_table(plan), y_table(plan)
    lines, base, x_inverse, y_inverse = lax.optimization_barrier(
        (lines, base, x_inverse, y_inverse)
    )
    modes = call(
        ry,
        to_modes,
        plan,
        shape((rx, kxd, plan.pairs, c, LANES), bf16),
        scratch=[pltpu.VMEM((2 * (plan.mx // 2 + 1) * cx, LANES), f32)],
    )(*lines)
    modes = exchange(modes)
    mixed = call(
        2,
        mix,
        plan,
        shape((rx, kyd, kxd, 2, b, LANES), bf16),
        scratch=[pltpu.VMEM((kyd, kxd, 2, b, LANES), f32)],
    )(modes, spectral)
    mixed = exchange(mixed)
    held = call(2, from_kx, plan, shape((cx, kyd, 2, b, LANES), bf16))(mixed, x_inverse)
    parts = [swap(held, k) for k in range(ry)]
    out = call(
        ry + 3,
        finish,
        plan,
        shape((b, plan.per, cx, cy, nz), bf16),
        scratch=[pltpu.VMEM((cx, b, plan.per, cy, nz), bf16), pltpu.SemaphoreType.DMA((cx,))],
        outer=(pltpu.VMEM, pl.ANY),
    )(*parts, base.reshape(b, plan.per, cx, cy, nz), y_inverse, z_table(plan))
    return out.reshape(c, cx, cy, nz)


def solution(mesh):
    in_specs = (
        P(None, "gx", "gy", None),
        P("gx", "gy", None),
        P("gx", "gy", None, None, None),
        P(),
        P(),
    )
    out_specs = P(None, "gx", "gy", None)
    return jax.shard_map(
        on_device, mesh=mesh, in_specs=in_specs, out_specs=out_specs, check_vma=False
    )
```

```python
import functools
import math

import jax
import jax.numpy as jnp
import numpy as np
from jax import lax
from jax.experimental import pallas as pl
from jax.experimental.pallas import tpu as pltpu
from jax.sharding import PartitionSpec as P


LANES = 128
GROUP = LANES // 2
QUARTER = LANES // 4


class Plan:
    def __init__(self, ranks_x, ranks_y, inputs, spectral):
        self.rx, self.ry = ranks_x, ranks_y
        self.c, self.cx, self.cy, self.nz = inputs.shape
        self.kxd, self.kyd = spectral.shape[:2]
        self.mz = spectral.shape[4] // self.c
        self.nx, self.ny = self.cx * ranks_x, self.cy * ranks_y
        self.mx, self.my = self.kxd * ranks_x, self.kyd * ranks_y
        self.pairs = self.kyd // 2
        self.blocks = self.c * self.mz // LANES
        self.per = LANES // self.mz
        first = ranks_x // 4
        self.order = [first] + [i for i in range(ranks_x) if i != first]
        assert self.nz == LANES and self.mz == QUARTER and self.kyd % 2 == 0
        assert ranks_y & (ranks_y - 1) == 0 and self.blocks == 8 and self.cy == 8


def dot(a, b):
    return jnp.dot(a, b, preferred_element_type=jnp.float32)


def iota(shape, axis):
    return lax.broadcasted_iota(jnp.int32, shape, axis)


def wave(winding, length):
    return jnp.cos(2.0 * math.pi / length * (winding % length).astype(jnp.float32))


def prepare(plan, waves_ref, forward_ref, regroup_ref):
    cy, ny, size = plan.cy, plan.ny, plan.c * plan.cy
    mine = lax.axis_index("gy")
    row, lane = iota(waves_ref.shape, 0), iota(waves_ref.shape, 1)
    winding = row // cy * (mine * cy + row % cy) - lane // GROUP * (ny // 4)
    waves_ref[...] = wave(winding + ny, ny)
    z, lane = iota((LANES, LANES), 0), iota((LANES, LANES), 1)
    turn = (lane // QUARTER + 1) // 2 * (plan.nz // 4)
    forward_ref[...] = wave(z * (lane % QUARTER) + turn, plan.nz).astype(jnp.bfloat16)
    row, column = iota((size, size), 0), iota((size, size), 1)
    same = row % plan.c * cy + row // plan.c == column
    regroup_ref[...] = same.astype(jnp.float32).astype(jnp.bfloat16)


def to_partial(plan, x_ref, waves, forward_ref, regroup_ref, *refs):
    outs, (pieces,) = refs[: plan.ry], refs[plan.ry :]
    c, cx, cy = plan.c, plan.cx, plan.cy
    size, half = c * cy, plan.my // 2
    mine = lax.axis_index("gy")
    forward, regroup = forward_ref[...], regroup_ref[...]
    low = iota((c // 2, LANES), 1) < GROUP
    for x in range(0, cx, 2):
        pair = [x_ref[:, x + i].reshape(size, LANES) for i in range(2)]
        pair = dot(regroup, jnp.concatenate(pair, axis=1)).astype(jnp.bfloat16)
        for i in range(2):
            spectrum = dot(pair[:, i * LANES : (i + 1) * LANES], forward)
            for part in range(2):
                begin = part * (c // 2)
                planes = [spectrum[y * c + begin : y * c + begin + c // 2] for y in range(cy)]
                sums = []
                for k in range(half + 1):
                    total = None
                    for y in range(cy):
                        term = waves[pl.ds(k * cy + y, 1), :] * planes[y]
                        total = term if total is None else total + term
                    sums.append((total, pltpu.roll(total, GROUP, 1)))
                for t in range(plan.my // 2):
                    sides = []
                    for side, j in enumerate((2 * t, 2 * t + 1)):
                        if j < half:
                            a, b = sums[j]
                            sides.append(a + b)
                        else:
                            a, b = sums[plan.my - j]
                            sides.append(b - a if side else a - b)
                    value = jnp.where(low, sides[0], sides[1]).astype(jnp.bfloat16)
                    pieces[t // plan.pairs, t % plan.pairs, x + i, pl.ds(begin, c // 2)] = value
    for k in range(plan.ry):
        outs[k][...] = pieces[mine ^ k]


def to_modes(plan, *refs):
    parts, (out_ref, waves) = refs[: plan.ry], refs[plan.ry :]
    c, cx, nx = plan.c, plan.cx, plan.nx
    half = plan.mx // 2
    count = (half + 1) * cx
    row = iota((2 * count, LANES), 0)
    place = lax.axis_index("gx") * cx + row % cx
    winding = row // cx % (half + 1) * place - row // count * (nx // 4)
    waves[...] = wave(winding + nx, nx)
    real = iota((c, LANES), 1) % GROUP < QUARTER
    for p in range(plan.pairs):
        lines, turned = [], []
        for x in range(cx):
            line = sum(part[p, x].astype(jnp.float32) for part in parts)
            lines.append(line)
            up, down = pltpu.roll(line, LANES - QUARTER, 1), pltpu.roll(line, QUARTER, 1)
            turned.append(jnp.where(real, up, -down))
        for k in range(half + 1):
            even = odd = None
            for x in range(cx):
                cosine = waves[pl.ds(k * cx + x, 1), :] * lines[x]
                sine = waves[pl.ds(count + k * cx + x, 1), :] * turned[x]
                even = cosine if even is None else even + cosine
                odd = sine if odd is None else odd + sine
            if k < half:
                owner = plan.order.index(k // plan.kxd)
                out_ref[owner, k % plan.kxd, p] = (even + odd).astype(jnp.bfloat16)
            if k > 0:
                back = plan.mx - k
                owner = plan.order.index(back // plan.kxd)
                out_ref[owner, back % plan.kxd, p] = (even - odd).astype(jnp.bfloat16)


def mix(plan, u_ref, w_ref, out_ref, sums):
    c = plan.c
    scale = 1.0 / math.sqrt(plan.nx * plan.ny * plan.nz)
    group = iota((c, LANES), 1) // QUARTER
    for kx in range(plan.kxd):
        for p in range(plan.pairs):
            u = sum(u_ref[r, kx, p].astype(jnp.float32) for r in range(plan.rx)) * scale
            rolled = [u] + [pltpu.roll(u, v * QUARTER, 1) for v in range(1, 4)]

            def spread(g):
                value = rolled[(3 - g) % 4]
                for j in (2, 1, 0):
                    value = jnp.where(group == j, rolled[(j - g) % 4], value)
                return value

            for side in range(2):
                ky = 2 * p + side
                u_real, u_imag = spread(2 * side), spread(2 * side + 1)
                for j in range(plan.blocks):
                    at = pl.ds(j * LANES, LANES)
                    w_real = w_ref[kx, ky, 0, :, at].astype(jnp.float32)
                    w_imag = w_ref[kx, ky, 1, :, at].astype(jnp.float32)
                    y_real = jnp.sum(w_real * u_real - w_imag * u_imag, axis=0, keepdims=True)
                    y_imag = jnp.sum(w_real * u_imag + w_imag * u_real, axis=0, keepdims=True)
                    sums[ky, kx, 0, pl.ds(j, 1), :] = y_real
                    sums[ky, kx, 1, pl.ds(j, 1), :] = y_imag
    mixed = sums[...].astype(jnp.bfloat16)
    for r in range(plan.rx):
        out_ref[r] = mixed


def from_kx(plan, m_ref, t_ref, out_ref):
    depth = plan.rx * plan.kxd * 2 * plan.blocks
    for ky in range(plan.kyd):
        lines = dot(t_ref[...], m_ref[:, ky].reshape(depth, LANES))
        lines = lines.reshape(plan.cx, 2, plan.blocks, LANES)
        out_ref[:, ky] = lines.astype(jnp.bfloat16)


def local_terms(plan, x_ref, d_ref, p_ref, o_ref, out_ref):
    c, cy = plan.c, plan.cy
    size = c * cy
    row = iota((size, c), 0) // cy
    pick = (row == iota((size, c), 1)).astype(jnp.bfloat16)
    spread = dot(pick, p_ref[...]).astype(jnp.bfloat16)
    wide = lax.dot_general(
        spread, pick, (((1,), (1,)), ((), ())), preferred_element_type=jnp.float32
    )
    same = iota((size, size), 0) % cy == iota((size, size), 1) % cy
    mixer = jnp.where(same, wide, 0.0).astype(jnp.bfloat16)
    lane = iota((size, LANES), 1)
    for x in range(plan.cx):
        v = x_ref[:, x].reshape(size, LANES)
        mixing = dot(mixer, v)
        f = v.astype(jnp.float32)
        before = jnp.where(lane == 0, 0.0, pltpu.roll(f, 1, 1))
        after = jnp.where(lane == LANES - 1, 0.0, pltpu.roll(f, LANES - 1, 1))
        curvature = (before + after - 2.0 * f).reshape(c, cy, LANES)
        d = d_ref[x].astype(jnp.float32)
        out_ref[:, x] = mixing.reshape(c, cy, LANES) + d[None] * curvature + o_ref[...]


def finish(plan, *refs):
    parts, (b_ref, y_ref, z_ref, out_hbm, held_out, sems) = refs[: plan.ry], refs[plan.ry :]
    size = plan.kyd * 2 * plan.blocks
    half, cy = plan.blocks * plan.cy, plan.cy
    lines = []
    for x in range(plan.cx):
        held = jnp.concatenate([part[x].reshape(size, LANES) for part in parts], axis=0)
        line = dot(y_ref[...], held)
        lines.append(jnp.concatenate([line[:half], line[half:]], axis=1))
    copies = []
    for j in range(plan.blocks):
        rows = jnp.concatenate([line[j * cy : (j + 1) * cy] for line in lines], axis=0)
        spectral = dot(rows.astype(jnp.bfloat16), z_ref[...])
        for o in range(plan.per):
            v = spectral[:, o * LANES : (o + 1) * LANES].reshape(plan.cx, cy, LANES)
            v = v + b_ref[j, o]
            gelu = 0.5 * v * (1.0 + lax.erf(v * math.sqrt(0.5)))
            held_out[j, o] = gelu.astype(jnp.bfloat16)
        copies.append(pltpu.make_async_copy(held_out.at[j], out_hbm.at[j], sems.at[j]))
        copies[-1].start()
    for copy in copies:
        copy.wait()


def x_table(plan):
    b = plan.blocks
    shape = (plan.cx * 2 * b, plan.rx * plan.kxd * 2 * b)
    row, column = iota(shape, 0), iota(shape, 1)
    order = jnp.asarray(plan.order, jnp.int32)[jnp.arange(shape[1]) // (plan.kxd * 2 * b)]
    kx = order[None, :] * plan.kxd + column // (2 * b) % plan.kxd
    kx = jnp.where(kx < plan.mx // 2, kx, kx - plan.mx)
    x = lax.axis_index("gx") * plan.cx + row // (2 * b)
    turn = (column // b % 2 - row // b % 2) * (plan.nx // 4)
    winding = kx * x + turn + plan.nx * plan.nx
    return jnp.where(row % b == column % b, wave(winding, plan.nx), 0.0).astype(jnp.bfloat16)


def y_table(plan):
    b, cy = plan.blocks, plan.cy
    shape = (2 * b * cy, plan.ry * plan.kyd * 2 * b)
    row, column = iota(shape, 0), iota(shape, 1)
    rank = column // (plan.kyd * 2 * b) ^ lax.axis_index("gy")
    ky = rank * plan.kyd + column // (2 * b) % plan.kyd
    ky = jnp.where(ky < plan.my // 2, ky, ky - plan.my)
    y = lax.axis_index("gy") * cy + row % cy
    turn = (column // b % 2 - row // (b * cy)) * (plan.ny // 4)
    winding = ky * y + turn + plan.ny * plan.ny
    return jnp.where(row // cy % b == column % b, wave(winding, plan.ny), 0.0).astype(jnp.bfloat16)


def z_table(plan):
    row = np.arange(2 * LANES)[:, None]
    column = np.arange(plan.per * LANES)[None, :]
    angle = 2.0 * np.pi / plan.nz * (row % plan.mz * column % plan.nz)
    value = np.where(row < LANES, np.cos(angle), -np.sin(angle))
    value = value / math.sqrt(plan.mx * plan.my * plan.mz)
    value = np.where(row % LANES // plan.mz == column // LANES, value, 0.0)
    return jnp.asarray(value.astype(np.float32).astype(jnp.bfloat16))


def call(n, body, plan, out, scratch=(), flops=0, moved=0, outer=(pltpu.VMEM, pltpu.VMEM)):
    near = pl.BlockSpec(memory_space=outer[0])
    vmem = pl.BlockSpec(memory_space=outer[1])
    return pl.pallas_call(
        functools.partial(body, plan),
        out_shape=out,
        in_specs=[near] * n,
        out_specs=jax.tree.map(lambda _: vmem, out),
        compiler_params=pltpu.CompilerParams(vmem_limit_bytes=16 * 2**20),
        scratch_shapes=list(scratch),
        cost_estimate=pl.CostEstimate(flops=flops, bytes_accessed=moved, transcendentals=0),
    )


def on_device(inputs, diffusion, spectral, pointwise, offsets):
    plan = Plan(lax.axis_size("gx"), lax.axis_size("gy"), inputs, spectral)
    c, cx, cy, nz = inputs.shape
    rx, ry, kxd, kyd, b = plan.rx, plan.ry, plan.kxd, plan.kyd, plan.blocks
    bf16, f32 = jnp.bfloat16, jnp.float32
    shape = jax.ShapeDtypeStruct
    order = [plan.order]

    def swap(value, k):
        if k == 0:
            return value
        return lax.ppermute(value, "gy", [(i, i ^ k) for i in range(ry)])

    def exchange(value):
        return lax.all_to_all(
            value, "gx", split_axis=0, concat_axis=0, axis_index_groups=order, tiled=True
        )

    size = c * cy
    tables = call(
        0,
        prepare,
        plan,
        [
            shape(((plan.my // 2 + 1) * cy, LANES), f32),
            shape((LANES, LANES), bf16),
            shape((size, size), bf16),
        ],
        flops=10**9,
        moved=4 * 10**6,
    )()
    partial = call(
        4,
        to_partial,
        plan,
        [shape((plan.pairs, cx, c, LANES), bf16)] * ry,
        scratch=[pltpu.VMEM((ry, plan.pairs, cx, c, LANES), bf16)],
    )(inputs, *tables)
    lines = [swap(partial[k], k) for k in range(ry)]
    base = call(4, local_terms, plan, shape((c, cx, cy, nz), f32), flops=10**9, moved=10**6)(
        inputs, diffusion, pointwise, jnp.broadcast_to(offsets[:, None, None], (c, cy, LANES))
    )
    x_inverse, y_inverse = x_table(plan), y_table(plan)
    lines, base, x_inverse, y_inverse = lax.optimization_barrier(
        (lines, base, x_inverse, y_inverse)
    )
    modes = call(
        ry,
        to_modes,
        plan,
        shape((rx, kxd, plan.pairs, c, LANES), bf16),
        scratch=[pltpu.VMEM((2 * (plan.mx // 2 + 1) * cx, LANES), f32)],
    )(*lines)
    modes = exchange(modes)
    mixed = call(
        2,
        mix,
        plan,
        shape((rx, kyd, kxd, 2, b, LANES), bf16),
        scratch=[pltpu.VMEM((kyd, kxd, 2, b, LANES), f32)],
    )(modes, spectral)
    mixed = exchange(mixed)
    held = call(2, from_kx, plan, shape((cx, kyd, 2, b, LANES), bf16))(mixed, x_inverse)
    parts = [swap(held, k) for k in range(ry)]
    out = call(
        ry + 3,
        finish,
        plan,
        shape((b, plan.per, cx, cy, nz), bf16),
        scratch=[pltpu.VMEM((b, plan.per, cx, cy, nz), bf16), pltpu.SemaphoreType.DMA((b,))],
        outer=(pltpu.VMEM, pl.ANY),
    )(*parts, base.reshape(b, plan.per, cx, cy, nz), y_inverse, z_table(plan))
    return out.reshape(c, cx, cy, nz)


def solution(mesh):
    in_specs = (
        P(None, "gx", "gy", None),
        P("gx", "gy", None),
        P("gx", "gy", None, None, None),
        P(),
        P(),
    )
    out_specs = P(None, "gx", "gy", None)
    return jax.shard_map(
        on_device, mesh=mesh, in_specs=in_specs, out_specs=out_specs, check_vma=False
    )
```

```python
import functools
import math

import jax
import jax.numpy as jnp
import numpy as np
from jax import lax
from jax.experimental import pallas as pl
from jax.experimental.pallas import tpu as pltpu
from jax.sharding import PartitionSpec as P


LANES = 128
GROUP = LANES // 2
QUARTER = LANES // 4


class Plan:
    def __init__(self, ranks_x, ranks_y, inputs, spectral):
        self.rx, self.ry = ranks_x, ranks_y
        self.c, self.cx, self.cy, self.nz = inputs.shape
        self.kxd, self.kyd = spectral.shape[:2]
        self.mz = spectral.shape[4] // self.c
        self.nx, self.ny = self.cx * ranks_x, self.cy * ranks_y
        self.mx, self.my = self.kxd * ranks_x, self.kyd * ranks_y
        self.pairs = self.kyd // 2
        self.blocks = self.c * self.mz // LANES
        self.per = LANES // self.mz
        first = ranks_x // 2 + 1
        self.order = [first] + [i for i in range(ranks_x) if i != first]
        assert self.nz == LANES and self.mz == QUARTER and self.kyd % 2 == 0
        assert ranks_y & (ranks_y - 1) == 0 and self.blocks == 8 and self.cy == 8


def dot(a, b):
    return jnp.dot(a, b, preferred_element_type=jnp.float32)


def iota(shape, axis):
    return lax.broadcasted_iota(jnp.int32, shape, axis)


def wave(winding, length):
    return jnp.cos(2.0 * math.pi / length * (winding % length).astype(jnp.float32))


def prepare(plan, waves_ref, forward_ref, regroup_ref):
    cy, ny, size = plan.cy, plan.ny, plan.c * plan.cy
    mine = lax.axis_index("gy")
    row, lane = iota(waves_ref.shape, 0), iota(waves_ref.shape, 1)
    winding = row // cy * (mine * cy + row % cy) - lane // GROUP * (ny // 4)
    waves_ref[...] = wave(winding + ny, ny)
    z, lane = iota((LANES, LANES), 0), iota((LANES, LANES), 1)
    turn = (lane // QUARTER + 1) // 2 * (plan.nz // 4)
    forward_ref[...] = wave(z * (lane % QUARTER) + turn, plan.nz).astype(jnp.bfloat16)
    row, column = iota((size, size), 0), iota((size, size), 1)
    same = row % plan.c * cy + row // plan.c == column
    regroup_ref[...] = same.astype(jnp.float32).astype(jnp.bfloat16)


def to_partial(plan, x_ref, waves, forward_ref, regroup_ref, *refs):
    outs, (pieces,) = refs[: plan.ry], refs[plan.ry :]
    c, cx, cy = plan.c, plan.cx, plan.cy
    size, half = c * cy, plan.my // 2
    mine = lax.axis_index("gy")
    forward, regroup = forward_ref[...], regroup_ref[...]
    low = iota((c // 2, LANES), 1) < GROUP
    for x in range(0, cx, 2):
        pair = [x_ref[:, x + i].reshape(size, LANES) for i in range(2)]
        pair = dot(regroup, jnp.concatenate(pair, axis=1)).astype(jnp.bfloat16)
        for i in range(2):
            spectrum = dot(pair[:, i * LANES : (i + 1) * LANES], forward)
            for part in range(2):
                begin = part * (c // 2)
                planes = [spectrum[y * c + begin : y * c + begin + c // 2] for y in range(cy)]
                sums = []
                for k in range(half + 1):
                    total = None
                    for y in range(cy):
                        term = waves[pl.ds(k * cy + y, 1), :] * planes[y]
                        total = term if total is None else total + term
                    sums.append((total, pltpu.roll(total, GROUP, 1)))
                for t in range(plan.my // 2):
                    sides = []
                    for side, j in enumerate((2 * t, 2 * t + 1)):
                        if j < half:
                            a, b = sums[j]
                            sides.append(a + b)
                        else:
                            a, b = sums[plan.my - j]
                            sides.append(b - a if side else a - b)
                    value = jnp.where(low, sides[0], sides[1]).astype(jnp.bfloat16)
                    pieces[t // plan.pairs, t % plan.pairs, x + i, pl.ds(begin, c // 2)] = value
    for k in range(plan.ry):
        outs[k][...] = pieces[mine ^ k]


def to_modes(plan, *refs):
    parts, (out_ref, waves) = refs[: plan.ry], refs[plan.ry :]
    c, cx, nx = plan.c, plan.cx, plan.nx
    half = plan.mx // 2
    count = (half + 1) * cx
    row = iota((2 * count, LANES), 0)
    place = lax.axis_index("gx") * cx + row % cx
    winding = row // cx % (half + 1) * place - row // count * (nx // 4)
    waves[...] = wave(winding + nx, nx)
    real = iota((c, LANES), 1) % GROUP < QUARTER
    for p in range(plan.pairs):
        lines, turned = [], []
        for x in range(cx):
            line = sum(part[p, x].astype(jnp.float32) for part in parts)
            lines.append(line)
            up, down = pltpu.roll(line, LANES - QUARTER, 1), pltpu.roll(line, QUARTER, 1)
            turned.append(jnp.where(real, up, -down))
        for k in range(half + 1):
            even = odd = None
            for x in range(cx):
                cosine = waves[pl.ds(k * cx + x, 1), :] * lines[x]
                sine = waves[pl.ds(count + k * cx + x, 1), :] * turned[x]
                even = cosine if even is None else even + cosine
                odd = sine if odd is None else odd + sine
            if k < half:
                owner = plan.order.index(k // plan.kxd)
                out_ref[owner, k % plan.kxd, p] = (even + odd).astype(jnp.bfloat16)
            if k > 0:
                back = plan.mx - k
                owner = plan.order.index(back // plan.kxd)
                out_ref[owner, back % plan.kxd, p] = (even - odd).astype(jnp.bfloat16)


def mix(plan, u_ref, w_ref, out_ref, sums):
    c = plan.c
    scale = 1.0 / math.sqrt(plan.nx * plan.ny * plan.nz)
    group = iota((c, LANES), 1) // QUARTER
    for kx in range(plan.kxd):
        for p in range(plan.pairs):
            u = sum(u_ref[r, kx, p].astype(jnp.float32) for r in range(plan.rx)) * scale
            rolled = [u] + [pltpu.roll(u, v * QUARTER, 1) for v in range(1, 4)]

            def spread(g):
                value = rolled[(3 - g) % 4]
                for j in (2, 1, 0):
                    value = jnp.where(group == j, rolled[(j - g) % 4], value)
                return value

            for side in range(2):
                ky = 2 * p + side
                u_real, u_imag = spread(2 * side), spread(2 * side + 1)
                for j in range(plan.blocks):
                    at = pl.ds(j * LANES, LANES)
                    w_real = w_ref[kx, ky, 0, :, at].astype(jnp.float32)
                    w_imag = w_ref[kx, ky, 1, :, at].astype(jnp.float32)
                    y_real = jnp.sum(w_real * u_real - w_imag * u_imag, axis=0, keepdims=True)
                    y_imag = jnp.sum(w_real * u_imag + w_imag * u_real, axis=0, keepdims=True)
                    sums[ky, kx, 0, pl.ds(j, 1), :] = y_real
                    sums[ky, kx, 1, pl.ds(j, 1), :] = y_imag
    mixed = sums[...].astype(jnp.bfloat16)
    for r in range(plan.rx):
        out_ref[r] = mixed


def from_kx(plan, m_ref, t_ref, out_ref):
    depth = plan.rx * plan.kxd * 2 * plan.blocks
    for ky in range(plan.kyd):
        lines = dot(t_ref[...], m_ref[:, ky].reshape(depth, LANES))
        lines = lines.reshape(plan.cx, 2, plan.blocks, LANES)
        out_ref[:, ky] = lines.astype(jnp.bfloat16)


def local_terms(plan, x_ref, d_ref, p_ref, o_ref, out_ref):
    c, cy = plan.c, plan.cy
    size = c * cy
    row = iota((size, c), 0) // cy
    pick = (row == iota((size, c), 1)).astype(jnp.bfloat16)
    spread = dot(pick, p_ref[...]).astype(jnp.bfloat16)
    wide = lax.dot_general(
        spread, pick, (((1,), (1,)), ((), ())), preferred_element_type=jnp.float32
    )
    same = iota((size, size), 0) % cy == iota((size, size), 1) % cy
    mixer = jnp.where(same, wide, 0.0).astype(jnp.bfloat16)
    lane = iota((size, LANES), 1)
    for x in range(plan.cx):
        v = x_ref[:, x].reshape(size, LANES)
        mixing = dot(mixer, v)
        f = v.astype(jnp.float32)
        before = jnp.where(lane == 0, 0.0, pltpu.roll(f, 1, 1))
        after = jnp.where(lane == LANES - 1, 0.0, pltpu.roll(f, LANES - 1, 1))
        curvature = (before + after - 2.0 * f).reshape(c, cy, LANES)
        d = d_ref[x].astype(jnp.float32)
        out_ref[:, x] = mixing.reshape(c, cy, LANES) + d[None] * curvature + o_ref[...]


def finish(plan, *refs):
    parts, (b_ref, y_ref, z_ref, out_hbm, held_out, sems) = refs[: plan.ry], refs[plan.ry :]
    size = plan.kyd * 2 * plan.blocks
    half, cy = plan.blocks * plan.cy, plan.cy
    lines = []
    for x in range(plan.cx):
        held = jnp.concatenate([part[x].reshape(size, LANES) for part in parts], axis=0)
        line = dot(y_ref[...], held)
        lines.append(jnp.concatenate([line[:half], line[half:]], axis=1))
    copies = []
    for j in range(plan.blocks):
        rows = jnp.concatenate([line[j * cy : (j + 1) * cy] for line in lines], axis=0)
        spectral = dot(rows.astype(jnp.bfloat16), z_ref[...])
        for o in range(plan.per):
            v = spectral[:, o * LANES : (o + 1) * LANES].reshape(plan.cx, cy, LANES)
            v = v + b_ref[j, o]
            gelu = 0.5 * v * (1.0 + lax.erf(v * math.sqrt(0.5)))
            held_out[j, o] = gelu.astype(jnp.bfloat16)
        copies.append(pltpu.make_async_copy(held_out.at[j], out_hbm.at[j], sems.at[j]))
        copies[-1].start()
    for copy in copies:
        copy.wait()


def x_table(plan):
    b = plan.blocks
    shape = (plan.cx * 2 * b, plan.rx * plan.kxd * 2 * b)
    row, column = iota(shape, 0), iota(shape, 1)
    order = jnp.asarray(plan.order, jnp.int32)[jnp.arange(shape[1]) // (plan.kxd * 2 * b)]
    kx = order[None, :] * plan.kxd + column // (2 * b) % plan.kxd
    kx = jnp.where(kx < plan.mx // 2, kx, kx - plan.mx)
    x = lax.axis_index("gx") * plan.cx + row // (2 * b)
    turn = (column // b % 2 - row // b % 2) * (plan.nx // 4)
    winding = kx * x + turn + plan.nx * plan.nx
    return jnp.where(row % b == column % b, wave(winding, plan.nx), 0.0).astype(jnp.bfloat16)


def y_table(plan):
    b, cy = plan.blocks, plan.cy
    shape = (2 * b * cy, plan.ry * plan.kyd * 2 * b)
    row, column = iota(shape, 0), iota(shape, 1)
    rank = column // (plan.kyd * 2 * b) ^ lax.axis_index("gy")
    ky = rank * plan.kyd + column // (2 * b) % plan.kyd
    ky = jnp.where(ky < plan.my // 2, ky, ky - plan.my)
    y = lax.axis_index("gy") * cy + row % cy
    turn = (column // b % 2 - row // (b * cy)) * (plan.ny // 4)
    winding = ky * y + turn + plan.ny * plan.ny
    return jnp.where(row // cy % b == column % b, wave(winding, plan.ny), 0.0).astype(jnp.bfloat16)


def z_table(plan):
    row = np.arange(2 * LANES)[:, None]
    column = np.arange(plan.per * LANES)[None, :]
    angle = 2.0 * np.pi / plan.nz * (row % plan.mz * column % plan.nz)
    value = np.where(row < LANES, np.cos(angle), -np.sin(angle))
    value = value / math.sqrt(plan.mx * plan.my * plan.mz)
    value = np.where(row % LANES // plan.mz == column // LANES, value, 0.0)
    return jnp.asarray(value.astype(np.float32).astype(jnp.bfloat16))


def call(n, body, plan, out, scratch=(), flops=0, moved=0, outer=(pltpu.VMEM, pltpu.VMEM)):
    near = pl.BlockSpec(memory_space=outer[0])
    vmem = pl.BlockSpec(memory_space=outer[1])
    return pl.pallas_call(
        functools.partial(body, plan),
        out_shape=out,
        in_specs=[near] * n,
        out_specs=jax.tree.map(lambda _: vmem, out),
        compiler_params=pltpu.CompilerParams(vmem_limit_bytes=16 * 2**20),
        scratch_shapes=list(scratch),
        cost_estimate=pl.CostEstimate(flops=flops, bytes_accessed=moved, transcendentals=0),
    )


def on_device(inputs, diffusion, spectral, pointwise, offsets):
    plan = Plan(lax.axis_size("gx"), lax.axis_size("gy"), inputs, spectral)
    c, cx, cy, nz = inputs.shape
    rx, ry, kxd, kyd, b = plan.rx, plan.ry, plan.kxd, plan.kyd, plan.blocks
    bf16, f32 = jnp.bfloat16, jnp.float32
    shape = jax.ShapeDtypeStruct
    order = [plan.order]

    def swap(value, k):
        if k == 0:
            return value
        return lax.ppermute(value, "gy", [(i, i ^ k) for i in range(ry)])

    def exchange(value):
        return lax.all_to_all(
            value, "gx", split_axis=0, concat_axis=0, axis_index_groups=order, tiled=True
        )

    size = c * cy
    tables = call(
        0,
        prepare,
        plan,
        [
            shape(((plan.my // 2 + 1) * cy, LANES), f32),
            shape((LANES, LANES), bf16),
            shape((size, size), bf16),
        ],
        flops=10**9,
        moved=4 * 10**6,
    )()
    partial = call(
        4,
        to_partial,
        plan,
        [shape((plan.pairs, cx, c, LANES), bf16)] * ry,
        scratch=[pltpu.VMEM((ry, plan.pairs, cx, c, LANES), bf16)],
    )(inputs, *tables)
    lines = [swap(partial[k], k) for k in range(ry)]
    base = call(4, local_terms, plan, shape((c, cx, cy, nz), f32), flops=10**9, moved=10**6)(
        inputs, diffusion, pointwise, jnp.broadcast_to(offsets[:, None, None], (c, cy, LANES))
    )
    x_inverse, y_inverse = x_table(plan), y_table(plan)
    lines, base, x_inverse, y_inverse = lax.optimization_barrier(
        (lines, base, x_inverse, y_inverse)
    )
    modes = call(
        ry,
        to_modes,
        plan,
        shape((rx, kxd, plan.pairs, c, LANES), bf16),
        scratch=[pltpu.VMEM((2 * (plan.mx // 2 + 1) * cx, LANES), f32)],
    )(*lines)
    modes = exchange(modes)
    mixed = call(
        2,
        mix,
        plan,
        shape((rx, kyd, kxd, 2, b, LANES), bf16),
        scratch=[pltpu.VMEM((kyd, kxd, 2, b, LANES), f32)],
    )(modes, spectral)
    mixed = exchange(mixed)
    held = call(2, from_kx, plan, shape((cx, kyd, 2, b, LANES), bf16))(mixed, x_inverse)
    across = swap(held, 3)
    parts = [held, swap(held, 1), swap(across, 1), across]
    out = call(
        ry + 3,
        finish,
        plan,
        shape((b, plan.per, cx, cy, nz), bf16),
        scratch=[pltpu.VMEM((b, plan.per, cx, cy, nz), bf16), pltpu.SemaphoreType.DMA((b,))],
        outer=(pltpu.VMEM, pl.ANY),
    )(*parts, base.reshape(b, plan.per, cx, cy, nz), y_inverse, z_table(plan))
    return out.reshape(c, cx, cy, nz)


def solution(mesh):
    in_specs = (
        P(None, "gx", "gy", None),
        P("gx", "gy", None),
        P("gx", "gy", None, None, None),
        P(),
        P(),
    )
    out_specs = P(None, "gx", "gy", None)
    return jax.shard_map(
        on_device, mesh=mesh, in_specs=in_specs, out_specs=out_specs, check_vma=False
    )
```

```python
import functools
import math

import jax
import jax.numpy as jnp
import numpy as np
from jax import lax
from jax.experimental import pallas as pl
from jax.experimental.pallas import tpu as pltpu
from jax.sharding import PartitionSpec as P


LANES = 128
GROUP = LANES // 2
QUARTER = LANES // 4


class Plan:
    def __init__(self, ranks_x, ranks_y, inputs, spectral):
        self.rx, self.ry = ranks_x, ranks_y
        self.c, self.cx, self.cy, self.nz = inputs.shape
        self.kxd, self.kyd = spectral.shape[:2]
        self.mz = spectral.shape[4] // self.c
        self.nx, self.ny = self.cx * ranks_x, self.cy * ranks_y
        self.mx, self.my = self.kxd * ranks_x, self.kyd * ranks_y
        self.pairs = self.kyd // 2
        self.blocks = self.c * self.mz // LANES
        self.per = LANES // self.mz
        first = ranks_x // 2 + 1
        self.order = [first] + [i for i in range(ranks_x) if i != first]
        assert self.nz == LANES and self.mz == QUARTER and self.kyd % 2 == 0
        assert ranks_y & (ranks_y - 1) == 0 and self.blocks == 8 and self.cy == 8


def dot(a, b):
    return jnp.dot(a, b, preferred_element_type=jnp.float32)


def iota(shape, axis):
    return lax.broadcasted_iota(jnp.int32, shape, axis)


def wave(winding, length):
    return jnp.cos(2.0 * math.pi / length * (winding % length).astype(jnp.float32))


def prepare(plan, waves_ref, forward_ref, regroup_ref):
    cy, ny, size = plan.cy, plan.ny, plan.c * plan.cy
    mine = lax.axis_index("gy")
    row, lane = iota(waves_ref.shape, 0), iota(waves_ref.shape, 1)
    winding = row // cy * (mine * cy + row % cy) - lane // GROUP * (ny // 4)
    waves_ref[...] = wave(winding + ny, ny)
    z, lane = iota((LANES, LANES), 0), iota((LANES, LANES), 1)
    turn = (lane // QUARTER + 1) // 2 * (plan.nz // 4)
    forward_ref[...] = wave(z * (lane % QUARTER) + turn, plan.nz).astype(jnp.bfloat16)
    row, column = iota((size, size), 0), iota((size, size), 1)
    same = row % plan.c * cy + row // plan.c == column
    regroup_ref[...] = same.astype(jnp.float32).astype(jnp.bfloat16)


def to_partial(plan, x_ref, waves, forward_ref, regroup_ref, *refs):
    outs, (pieces,) = refs[: plan.ry], refs[plan.ry :]
    c, cx, cy = plan.c, plan.cx, plan.cy
    size, half = c * cy, plan.my // 2
    mine = lax.axis_index("gy")
    forward, regroup = forward_ref[...], regroup_ref[...]
    low = iota((c // 2, LANES), 1) < GROUP
    for x in range(0, cx, 2):
        pair = [x_ref[:, x + i].reshape(size, LANES) for i in range(2)]
        pair = dot(regroup, jnp.concatenate(pair, axis=1)).astype(jnp.bfloat16)
        for i in range(2):
            spectrum = dot(pair[:, i * LANES : (i + 1) * LANES], forward)
            for part in range(2):
                begin = part * (c // 2)
                planes = [spectrum[y * c + begin : y * c + begin + c // 2] for y in range(cy)]
                sums = []
                for k in range(half + 1):
                    total = None
                    for y in range(cy):
                        term = waves[pl.ds(k * cy + y, 1), :] * planes[y]
                        total = term if total is None else total + term
                    sums.append((total, pltpu.roll(total, GROUP, 1)))
                for t in range(plan.my // 2):
                    sides = []
                    for side, j in enumerate((2 * t, 2 * t + 1)):
                        if j < half:
                            a, b = sums[j]
                            sides.append(a + b)
                        else:
                            a, b = sums[plan.my - j]
                            sides.append(b - a if side else a - b)
                    value = jnp.where(low, sides[0], sides[1]).astype(jnp.bfloat16)
                    pieces[t // plan.pairs, t % plan.pairs, x + i, pl.ds(begin, c // 2)] = value
    for k in range(plan.ry):
        outs[k][...] = pieces[mine ^ k]


def to_modes(plan, *refs):
    parts, (out_ref, waves) = refs[: plan.ry], refs[plan.ry :]
    c, cx, nx = plan.c, plan.cx, plan.nx
    half = plan.mx // 2
    count = (half + 1) * cx
    row = iota((2 * count, LANES), 0)
    place = lax.axis_index("gx") * cx + row % cx
    winding = row // cx % (half + 1) * place - row // count * (nx // 4)
    waves[...] = wave(winding + nx, nx)
    real = iota((c, LANES), 1) % GROUP < QUARTER
    for p in range(plan.pairs):
        lines, turned = [], []
        for x in range(cx):
            line = sum(part[p, x].astype(jnp.float32) for part in parts)
            lines.append(line)
            up, down = pltpu.roll(line, LANES - QUARTER, 1), pltpu.roll(line, QUARTER, 1)
            turned.append(jnp.where(real, up, -down))
        for k in range(half + 1):
            even = odd = None
            for x in range(cx):
                cosine = waves[pl.ds(k * cx + x, 1), :] * lines[x]
                sine = waves[pl.ds(count + k * cx + x, 1), :] * turned[x]
                even = cosine if even is None else even + cosine
                odd = sine if odd is None else odd + sine
            if k < half:
                owner = plan.order.index(k // plan.kxd)
                out_ref[owner, k % plan.kxd, p] = (even + odd).astype(jnp.bfloat16)
            if k > 0:
                back = plan.mx - k
                owner = plan.order.index(back // plan.kxd)
                out_ref[owner, back % plan.kxd, p] = (even - odd).astype(jnp.bfloat16)


def mix(plan, u_ref, w_ref, out_ref, sums):
    c = plan.c
    scale = 1.0 / math.sqrt(plan.nx * plan.ny * plan.nz)
    group = iota((c, LANES), 1) // QUARTER
    for kx in range(plan.kxd):
        for p in range(plan.pairs):
            u = sum(u_ref[r, kx, p].astype(jnp.float32) for r in range(plan.rx)) * scale
            rolled = [u] + [pltpu.roll(u, v * QUARTER, 1) for v in range(1, 4)]

            def spread(g):
                value = rolled[(3 - g) % 4]
                for j in (2, 1, 0):
                    value = jnp.where(group == j, rolled[(j - g) % 4], value)
                return value

            for side in range(2):
                ky = 2 * p + side
                u_real, u_imag = spread(2 * side), spread(2 * side + 1)
                u_sum, u_gap = u_real + u_imag, u_imag - u_real
                for j in range(plan.blocks):
                    at = pl.ds(j * LANES, LANES)
                    w_real = w_ref[kx, ky, 0, :, at].astype(jnp.float32)
                    w_imag = w_ref[kx, ky, 1, :, at].astype(jnp.float32)
                    both = jnp.sum((w_real + w_imag) * u_real, axis=0, keepdims=True)
                    y_real = both - jnp.sum(w_imag * u_sum, axis=0, keepdims=True)
                    y_imag = both + jnp.sum(w_real * u_gap, axis=0, keepdims=True)
                    sums[ky, kx, 0, pl.ds(j, 1), :] = y_real
                    sums[ky, kx, 1, pl.ds(j, 1), :] = y_imag
    mixed = sums[...].astype(jnp.bfloat16)
    for r in range(plan.rx):
        out_ref[r] = mixed


def from_kx(plan, m_ref, t_ref, out_ref):
    depth = plan.rx * plan.kxd * 2 * plan.blocks
    for ky in range(plan.kyd):
        lines = dot(t_ref[...], m_ref[:, ky].reshape(depth, LANES))
        lines = lines.reshape(plan.cx, 2, plan.blocks, LANES)
        out_ref[:, ky] = lines.astype(jnp.bfloat16)


def local_terms(plan, x_ref, d_ref, p_ref, o_ref, out_ref):
    c, cy = plan.c, plan.cy
    size = c * cy
    row = iota((size, c), 0) // cy
    pick = (row == iota((size, c), 1)).astype(jnp.bfloat16)
    spread = dot(pick, p_ref[...]).astype(jnp.bfloat16)
    wide = lax.dot_general(
        spread, pick, (((1,), (1,)), ((), ())), preferred_element_type=jnp.float32
    )
    same = iota((size, size), 0) % cy == iota((size, size), 1) % cy
    mixer = jnp.where(same, wide, 0.0).astype(jnp.bfloat16)
    lane = iota((size, LANES), 1)
    for x in range(plan.cx):
        v = x_ref[:, x].reshape(size, LANES)
        mixing = dot(mixer, v)
        f = v.astype(jnp.float32)
        before = jnp.where(lane == 0, 0.0, pltpu.roll(f, 1, 1))
        after = jnp.where(lane == LANES - 1, 0.0, pltpu.roll(f, LANES - 1, 1))
        curvature = (before + after - 2.0 * f).reshape(c, cy, LANES)
        d = d_ref[x].astype(jnp.float32)
        out_ref[:, x] = mixing.reshape(c, cy, LANES) + d[None] * curvature + o_ref[...]


def finish(plan, *refs):
    parts, (b_ref, y_ref, z_ref, out_hbm, held_out, sems) = refs[: plan.ry], refs[plan.ry :]
    size = plan.kyd * 2 * plan.blocks
    half, cy = plan.blocks * plan.cy, plan.cy
    lines = []
    for x in range(plan.cx):
        held = jnp.concatenate([part[x].reshape(size, LANES) for part in parts], axis=0)
        line = dot(y_ref[...], held)
        lines.append(jnp.concatenate([line[:half], line[half:]], axis=1))
    copies = []
    for j in range(plan.blocks):
        rows = jnp.concatenate([line[j * cy : (j + 1) * cy] for line in lines], axis=0)
        spectral = dot(rows.astype(jnp.bfloat16), z_ref[...])
        for o in range(plan.per):
            v = spectral[:, o * LANES : (o + 1) * LANES].reshape(plan.cx, cy, LANES)
            v = v + b_ref[j, o]
            gelu = 0.5 * v * (1.0 + lax.erf(v * math.sqrt(0.5)))
            held_out[j, o] = gelu.astype(jnp.bfloat16)
        copies.append(pltpu.make_async_copy(held_out.at[j], out_hbm.at[j], sems.at[j]))
        copies[-1].start()
    for copy in copies:
        copy.wait()


def x_table(plan):
    b = plan.blocks
    shape = (plan.cx * 2 * b, plan.rx * plan.kxd * 2 * b)
    row, column = iota(shape, 0), iota(shape, 1)
    order = jnp.asarray(plan.order, jnp.int32)[jnp.arange(shape[1]) // (plan.kxd * 2 * b)]
    kx = order[None, :] * plan.kxd + column // (2 * b) % plan.kxd
    kx = jnp.where(kx < plan.mx // 2, kx, kx - plan.mx)
    x = lax.axis_index("gx") * plan.cx + row // (2 * b)
    turn = (column // b % 2 - row // b % 2) * (plan.nx // 4)
    winding = kx * x + turn + plan.nx * plan.nx
    return jnp.where(row % b == column % b, wave(winding, plan.nx), 0.0).astype(jnp.bfloat16)


def y_table(plan):
    b, cy = plan.blocks, plan.cy
    shape = (2 * b * cy, plan.ry * plan.kyd * 2 * b)
    row, column = iota(shape, 0), iota(shape, 1)
    rank = column // (plan.kyd * 2 * b) ^ lax.axis_index("gy")
    ky = rank * plan.kyd + column // (2 * b) % plan.kyd
    ky = jnp.where(ky < plan.my // 2, ky, ky - plan.my)
    y = lax.axis_index("gy") * cy + row % cy
    turn = (column // b % 2 - row // (b * cy)) * (plan.ny // 4)
    winding = ky * y + turn + plan.ny * plan.ny
    return jnp.where(row // cy % b == column % b, wave(winding, plan.ny), 0.0).astype(jnp.bfloat16)


def z_table(plan):
    row = np.arange(2 * LANES)[:, None]
    column = np.arange(plan.per * LANES)[None, :]
    angle = 2.0 * np.pi / plan.nz * (row % plan.mz * column % plan.nz)
    value = np.where(row < LANES, np.cos(angle), -np.sin(angle))
    value = value / math.sqrt(plan.mx * plan.my * plan.mz)
    value = np.where(row % LANES // plan.mz == column // LANES, value, 0.0)
    return jnp.asarray(value.astype(np.float32).astype(jnp.bfloat16))


def call(n, body, plan, out, scratch=(), flops=0, moved=0, outer=(pltpu.VMEM, pltpu.VMEM)):
    near = pl.BlockSpec(memory_space=outer[0])
    vmem = pl.BlockSpec(memory_space=outer[1])
    return pl.pallas_call(
        functools.partial(body, plan),
        out_shape=out,
        in_specs=[near] * n,
        out_specs=jax.tree.map(lambda _: vmem, out),
        compiler_params=pltpu.CompilerParams(vmem_limit_bytes=16 * 2**20),
        scratch_shapes=list(scratch),
        cost_estimate=pl.CostEstimate(flops=flops, bytes_accessed=moved, transcendentals=0),
    )


def on_device(inputs, diffusion, spectral, pointwise, offsets):
    plan = Plan(lax.axis_size("gx"), lax.axis_size("gy"), inputs, spectral)
    c, cx, cy, nz = inputs.shape
    rx, ry, kxd, kyd, b = plan.rx, plan.ry, plan.kxd, plan.kyd, plan.blocks
    bf16, f32 = jnp.bfloat16, jnp.float32
    shape = jax.ShapeDtypeStruct
    order = [plan.order]

    def swap(value, k):
        if k == 0:
            return value
        return lax.ppermute(value, "gy", [(i, i ^ k) for i in range(ry)])

    def exchange(value):
        return lax.all_to_all(
            value, "gx", split_axis=0, concat_axis=0, axis_index_groups=order, tiled=True
        )

    size = c * cy
    tables = call(
        0,
        prepare,
        plan,
        [
            shape(((plan.my // 2 + 1) * cy, LANES), f32),
            shape((LANES, LANES), bf16),
            shape((size, size), bf16),
        ],
        flops=10**9,
        moved=4 * 10**6,
    )()
    partial = call(
        4,
        to_partial,
        plan,
        [shape((plan.pairs, cx, c, LANES), bf16)] * ry,
        scratch=[pltpu.VMEM((ry, plan.pairs, cx, c, LANES), bf16)],
    )(inputs, *tables)
    lines = [swap(partial[k], k) for k in range(ry)]
    base = call(4, local_terms, plan, shape((c, cx, cy, nz), f32), flops=10**9, moved=10**6)(
        inputs, diffusion, pointwise, jnp.broadcast_to(offsets[:, None, None], (c, cy, LANES))
    )
    x_inverse, y_inverse = x_table(plan), y_table(plan)
    lines, base, x_inverse, y_inverse = lax.optimization_barrier(
        (lines, base, x_inverse, y_inverse)
    )
    modes = call(
        ry,
        to_modes,
        plan,
        shape((rx, kxd, plan.pairs, c, LANES), bf16),
        scratch=[pltpu.VMEM((2 * (plan.mx // 2 + 1) * cx, LANES), f32)],
    )(*lines)
    modes = exchange(modes)
    mixed = call(
        2,
        mix,
        plan,
        shape((rx, kyd, kxd, 2, b, LANES), bf16),
        scratch=[pltpu.VMEM((kyd, kxd, 2, b, LANES), f32)],
    )(modes, spectral)
    mixed = exchange(mixed)
    held = call(2, from_kx, plan, shape((cx, kyd, 2, b, LANES), bf16))(mixed, x_inverse)
    across = swap(held, 3)
    parts = [held, swap(held, 1), swap(across, 1), across]
    out = call(
        ry + 3,
        finish,
        plan,
        shape((b, plan.per, cx, cy, nz), bf16),
        scratch=[pltpu.VMEM((b, plan.per, cx, cy, nz), bf16), pltpu.SemaphoreType.DMA((b,))],
        outer=(pltpu.VMEM, pl.ANY),
    )(*parts, base.reshape(b, plan.per, cx, cy, nz), y_inverse, z_table(plan))
    return out.reshape(c, cx, cy, nz)


def solution(mesh):
    in_specs = (
        P(None, "gx", "gy", None),
        P("gx", "gy", None),
        P("gx", "gy", None, None, None),
        P(),
        P(),
    )
    out_specs = P(None, "gx", "gy", None)
    return jax.shard_map(
        on_device, mesh=mesh, in_specs=in_specs, out_specs=out_specs, check_vma=False
    )
```
